256 devices in a mesh: slab: 32 (over x, y, core), orb: 8 (over z).
Axes of the slice: x: 4, y: 4, z: 8, core: 2. Of those that a mesh axis runs over, the one named last changes fastest.
Arguments:
- orbitals: float32 [256, 65536], P('orb', 'slab'), may hold values from -6 to 6
- cell_matrices: bfloat16 [256, 512, 512], P('slab'), as said below
- connectivity: int32 [256, 512], P('slab'), may hold values from 0 to 2559, as said below
- face_lower: int32 [8192], P('slab'), may hold values from 0 to 2047, as said below
- face_upper: int32 [8192], P('slab'), may hold values from 0 to 2047, as said below
Outputs:
- orthonormal_orbitals: float32 [256, 65536], P('orb', 'slab')
The draws below stay inside these ranges and needn't reach their ends.
Inputs may be any that keep to these rules, and one draw needn't show every extreme that they name: `connectivity`: each row names 512 distinct positions of its slab's extended numbering. `face_lower`: each slab's block of 256 entries names distinct own nodes; it shares no entry with the same slab's block of face_upper. `face_upper`: each slab's block of 256 entries names distinct own nodes; it shares no entry with the same slab's block of face_lower. `cell_matrices`: each cell matrix is symmetric.
All inputs are finite; a program needn't handle non-finite values.
Results may differ from the reference program's by a relative error of at most 0.023.
Values may be sent and summed in bfloat16 or wider, within the bound.
A program may use at most 64 MiB of HBM per device.

```python
import math
import jax
import jax.numpy as jnp
from jax import lax

ORBITALS = 256
CELL_NODES = 512
DEGREE = 4
CELL_DEV = 8
NODE_DEV = 2048
FACE = 256
EXT = 2560
SLABS = 32
CELLS = 256
NODES = 65536


def place_value(order_row, wanted, place_at):
    found = jnp.argmax(order_row == wanted)
    held = order_row[place_at]
    order_row = order_row.at[found].set(held)
    return order_row.at[place_at].set(wanted)


def face_maps(key):
    slab_keys = jax.random.split(jax.random.fold_in(key, 5), SLABS)
    orders = jax.vmap(lambda one_key: jax.random.permutation(one_key, NODE_DEV))(slab_keys).astype(jnp.int32)
    first_row = place_value(place_value(orders[0], NODE_DEV - 1, 0), 0, 1)
    second_row = place_value(place_value(orders[1], NODE_DEV - 1, FACE), 0, FACE + 1)
    orders = orders.at[0].set(first_row).at[1].set(second_row)
    return (orders[:, :FACE].reshape(-1), orders[:, FACE:2 * FACE].reshape(-1))


def draw_face_lower(key, part):
    return face_maps(key)[0].astype(jnp.int32)


def draw_face_upper(key, part):
    return face_maps(key)[1].astype(jnp.int32)


def draw_connectivity(key, part):
    cell_keys = jax.random.split(jax.random.fold_in(key, 11), CELLS)
    orders = jax.vmap(lambda one_key: jax.random.permutation(one_key, EXT))(cell_keys).astype(jnp.int32)
    first_row = place_value(place_value(orders[0], EXT - 1, 0), 0, 1)
    orders = orders.at[0].set(first_row)
    return orders[:, :CELL_NODES].astype(jnp.int32)


def draw_cell_matrices(key, part):
    spread_scale = 0.45 / math.sqrt(CELL_DEV * CELL_NODES * CELL_NODES / EXT)
    inner_key = jax.random.fold_in(key, 17)
    entries = jax.random.normal(inner_key, (CELLS, CELL_NODES, CELL_NODES), jnp.float32)
    symmetric = (entries + jnp.swapaxes(entries, 1, 2)) * (spread_scale / math.sqrt(2.0))
    return symmetric.astype(jnp.bfloat16)


def block_scale(own_key, dims, cuts, least, high):
    def one(position, parts):
        heights = jax.random.uniform(jax.random.fold_in(jax.random.fold_in(own_key, 6), position), (parts,), jnp.float32, least / len(cuts), high / len(cuts))
        return jnp.repeat(jnp.exp(heights), dims[position] // parts).reshape((-1,) + (1,) * (len(dims) - position - 1))

    level = one(*cuts[0])
    for cut in cuts[1:]:
        level = level * one(*cut)
    return level


def noise(stream_key, dims, scale, most, shards=(), kind=jnp.bfloat16):
    values = jax.random.normal(stream_key, dims, jnp.float32) * scale
    if len(shards) > 0:
        values = block_scale(stream_key, dims, shards, -0.22, 0.18) * values
    return jnp.clip(values, min=-most, max=most).astype(kind)


def setup_inputs(seed: int = 0) -> dict:
    keys = jax.random.split(jax.random.key(seed), 6)
    orbitals = noise(keys[0], (ORBITALS, NODES), 1.0, 6.0, ((0, 8), (1, 32)), jnp.float32)
    cell_matrices = draw_cell_matrices(jax.random.fold_in(keys[5], 71), 0)
    connectivity = draw_connectivity(jax.random.fold_in(keys[5], 71), 0)
    face_lower = draw_face_lower(jax.random.fold_in(keys[5], 71), 0)
    face_upper = draw_face_upper(jax.random.fold_in(keys[5], 71), 0)
    return {"orbitals": orbitals, "cell_matrices": cell_matrices, "connectivity": connectivity, "face_lower": face_lower, "face_upper": face_upper}


def global_cells(connectivity, face_lower, face_upper):
    lower_maps = face_lower.reshape(SLABS, FACE)
    upper_maps = face_upper.reshape(SLABS, FACE)
    slab_ids = jnp.arange(SLABS, dtype=jnp.int32)[:, None]
    missing = jnp.int32(NODES)
    below = jnp.where(slab_ids > 0, (slab_ids - 1) * NODE_DEV + jnp.roll(upper_maps, 1, axis=0), missing)
    owned = slab_ids * NODE_DEV + jnp.arange(NODE_DEV, dtype=jnp.int32)[None, :]
    above = jnp.where(slab_ids < SLABS - 1, (slab_ids + 1) * NODE_DEV + jnp.roll(lower_maps, -1, axis=0), missing)
    table = jnp.concatenate([below, owned, above], axis=1).astype(jnp.int32)
    local_cells = connectivity.reshape(SLABS, CELL_DEV * CELL_NODES).astype(jnp.int32)
    return jnp.take_along_axis(table, local_cells, axis=1).astype(jnp.int32)

def apply_hamiltonian(wave_field, cell_index, cell_matrices):
    padded = jnp.concatenate([wave_field.astype(jnp.bfloat16), jnp.zeros((ORBITALS, 1), jnp.bfloat16)], axis=1)
    matrices = cell_matrices.reshape(SLABS, CELL_DEV, CELL_NODES, CELL_NODES)

    def add_slab(summed, inputs):
        slab_index, slab_blocks = inputs
        pieces = jnp.take(padded, slab_index, axis=1).reshape(ORBITALS, CELL_DEV, CELL_NODES).astype(jnp.float32)
        cell_terms = jnp.einsum('ocn,cnm->ocm', pieces, slab_blocks.astype(jnp.float32))
        return (summed.at[:, slab_index].add(cell_terms.reshape(ORBITALS, CELL_DEV * CELL_NODES)), None)
    summed, _ = lax.scan(add_slab, jnp.zeros((ORBITALS, NODES + 1), jnp.float32), (cell_index, matrices))
    return summed[:, :NODES]

def reference(orbitals, cell_matrices, connectivity, face_lower, face_upper):
    cell_index = global_cells(connectivity, face_lower, face_upper)
    previous = orbitals
    current = apply_hamiltonian(orbitals, cell_index, cell_matrices)
    for degree_step in range(1, DEGREE):
        following = 2.0 * apply_hamiltonian(current, cell_index, cell_matrices) - previous
        previous, current = (current, following)
    gram = jnp.dot(current, current.T, precision=lax.Precision.HIGHEST)
    factor = jnp.linalg.cholesky(gram)
    solved = lax.linalg.triangular_solve(factor, current, left_side=True, lower=True)
    return solved * math.sqrt(NODES)
```

```python
import functools
import math

import jax
import jax.numpy as jnp
from jax import lax
from jax.experimental import pallas as pl
from jax.experimental.pallas import tpu as pltpu
from jax.sharding import PartitionSpec as P

MESH = pl.DeviceIdType.MESH
F32, BF16 = jnp.float32, jnp.bfloat16
HIGHEST = lax.Precision.HIGHEST
NT = (((1,), (1,)), ((), ()))
TN = (((0,), (0,)), ((), ()))

DEGREE = 4
CELLS = 8
LOCAL = 512
ROWS = 32
OWN = 2048
FACE = 256
BLOCKS = 8
SLABS = 32
SIDE = 4
PIECES = 4
PIECE = OWN // PIECES
HALF = ROWS // 2
ALL = ROWS * BLOCKS


def one_hot(first, wanted, rows):
    numbers = lax.broadcasted_iota(jnp.int32, (rows, wanted.shape[1]), 0)
    return jnp.where(numbers == wanted - first, 1.0, 0.0).astype(BF16)


def eliminate(block):
    row_id = lax.broadcasted_iota(jnp.int32, (ROWS, ROWS), 0)
    column_id = lax.broadcasted_iota(jnp.int32, (ROWS, ROWS), 1)
    work = jnp.concatenate([block, (row_id == column_id).astype(F32)], axis=1)
    below = lax.broadcasted_iota(jnp.int32, (ROWS, 1), 0)
    for j in range(ROWS):
        scaled = work[j : j + 1, :] / work[j : j + 1, j : j + 1]
        work = work - jnp.where(below > j, work[:, j : j + 1], 0.0) * scaled
    pivots = jnp.sum(jnp.where(row_id == column_id, work[:, :ROWS], 0.0), axis=1, keepdims=True)
    return work[:, ROWS:] * lax.rsqrt(pivots)


def invert_factor(gram, inverse):
    lane = lax.broadcasted_iota(jnp.int32, (ROWS, ALL), 1)
    row = lax.broadcasted_iota(jnp.int32, (ROWS, ALL), 0)
    for b in range(BLOCKS):
        low, high = b * ROWS, (b + 1) * ROWS
        diagonal = eliminate(gram[low:high, low:high])
        here = (lane >= low) & (lane < high)
        strip = jnp.where(here, (lane - low == row).astype(F32), gram[low:high, :])
        strip = jnp.dot(diagonal, strip, precision=HIGHEST, preferred_element_type=F32)
        inverse[b] = jnp.where(lane < high, strip, 0.0)
        if b < BLOCKS - 1:
            update = lax.dot_general(
                strip[:, high:], strip, TN, precision=HIGHEST, preferred_element_type=F32
            )
            rest = gram[high:, :]
            lanes = lax.broadcasted_iota(jnp.int32, rest.shape, 1)
            gram[high:, :] = jnp.where((lanes >= low) & (lanes < high), 0.0, rest) - update


def kernel(
    orbitals, connectivity, faces, matrices_hbm, out,
    picker, face_table, matrices, field_a, field_b, rounded, pieces, terms,
    halo, halo_out, back, back_out, blocks, halves, half_in, along_x, along_y, rows_all,
    gram, inverse,
    load_sem, halo_ssem, halo_rsem, back_ssem, back_rsem, ring_ssem, ring_rsem,
    core_ssem, core_rsem, x_ssem, x_rsem, y_ssem, y_rsem, z_ssem, z_rsem, pair_ssem, pair_rsem,
):
    s, o = lax.axis_index("slab"), lax.axis_index("orb")
    core, y, x = lax.rem(s, 2), lax.rem(s // 2, SIDE), s // (2 * SIDE)
    other_core = s + 1 - 2 * core

    load = pltpu.make_async_copy(matrices_hbm, matrices, load_sem)
    load.start()

    def slab_of(x_at, y_at, core_at):
        return (x_at * SIDE + y_at) * 2 + core_at

    def copy(source, target, ssem, rsem, **device):
        return pltpu.make_async_remote_copy(
            src_ref=source, dst_ref=target, send_sem=ssem, recv_sem=rsem,
            device_id=device, device_id_type=MESH,
        )

    up, down = lax.rem(s + 1, SLABS), lax.rem(s + SLABS - 1, SLABS)
    has = (s > 0, s < SLABS - 1)
    neighbour = (down, up)

    halo[...] = jnp.zeros_like(halo)
    back[...] = jnp.zeros_like(back)

    barrier = pltpu.get_barrier_semaphore()
    for d in range(1, BLOCKS):
        pl.semaphore_signal(
            barrier, inc=1, device_id={"orb": lax.rem(o + d, BLOCKS)}, device_id_type=MESH
        )
    for d in range(1, SIDE):
        for there in (
            slab_of(lax.rem(x + d, SIDE), y, core),
            slab_of(x, lax.rem(y + d, SIDE), core),
        ):
            pl.semaphore_signal(barrier, inc=1, device_id={"slab": there}, device_id_type=MESH)
    for there in neighbour:
        pl.semaphore_signal(barrier, inc=1, device_id={"slab": there}, device_id_type=MESH)

    face_table[...] = one_hot(0, faces[...], OWN)
    field_a[...] = orbitals[...]
    rounded[...] = orbitals[...].astype(BF16)

    pl.semaphore_wait(barrier, BLOCKS - 1 + 2 * (SIDE - 1) + 2)

    def exchange(k, sent, received, ssem, rsem):
        return [
            copy(
                sent.at[k, side], received.at[k, 1 - side],
                ssem.at[k, side], rsem.at[k, 1 - side], slab=neighbour[side],
            )
            for side in range(2)
        ]

    def start_both(copies):
        for side in range(2):
            pl.when(has[side])(copies[side].start)

    def land_both(copies):
        for side in range(2):
            pl.when(has[side])(copies[1 - side].wait_recv)

    def leave_both(copies):
        for side in range(2):
            pl.when(has[side])(copies[side].wait_send)

    def send_faces(k):
        values = jnp.dot(rounded[...], face_table[...], preferred_element_type=F32).astype(BF16)
        halo_out[k, 0] = values[:, :FACE]
        halo_out[k, 1] = values[:, FACE:]
        copies = exchange(k, halo_out, halo, halo_ssem, halo_rsem)
        start_both(copies)
        return copies

    fields = [field_a, field_b]
    for k in range(DEGREE):
        halo_copies = send_faces(k)
        if k == 0:

            def build(c, _):
                wanted = connectivity[pl.ds(c, 1), :]
                for t in range(OWN // FACE):
                    picker[c, t * FACE : (t + 1) * FACE, :] = one_hot(FACE + t * FACE, wanted, FACE)
                picker[c, OWN : OWN + FACE, :] = one_hot(0, wanted, FACE)
                picker[c, OWN + FACE :, :] = one_hot(OWN + FACE, wanted, FACE)
                return 0

            lax.fori_loop(0, CELLS, build, 0)

        def gather_own(c, _):
            pieces[c] = jnp.dot(
                rounded[...], picker[c, :OWN, :], preferred_element_type=F32
            ).astype(BF16)
            return 0

        lax.fori_loop(0, CELLS, gather_own, 0)
        if k == 0:
            load.wait()
        land_both(halo_copies)
        from_sides = jnp.concatenate([halo[k, 0], halo[k, 1]], axis=1)

        def cell(c, face_sum):
            shared = picker[c, OWN:, :]
            values = pieces[c].astype(F32) + jnp.dot(
                from_sides, shared, preferred_element_type=F32
            )
            term = jnp.dot(
                values.astype(BF16), matrices[c], preferred_element_type=F32
            ).astype(BF16)
            terms[c] = term
            return face_sum + lax.dot_general(term, shared, NT, preferred_element_type=F32)

        face_sum = lax.fori_loop(0, CELLS, cell, jnp.zeros((ROWS, 2 * FACE), F32))
        back_out[k, 0] = face_sum[:, :FACE].astype(BF16)
        back_out[k, 1] = face_sum[:, FACE:].astype(BF16)
        back_copies = exchange(k, back_out, back, back_ssem, back_rsem)
        start_both(back_copies)

        target = fields[(k + 1) % 2]

        def scatter_own(t, _):
            columns = pl.ds(pl.multiple_of(t * FACE, FACE), FACE)
            total = jnp.zeros((ROWS, FACE), F32)
            for c in range(CELLS):
                total += lax.dot_general(
                    terms[c], picker[c, columns, :], NT, preferred_element_type=F32
                )
            if k == 0:
                target[:, columns] = total
            else:
                target[:, columns] = 2.0 * total - target[:, columns]
            return 0

        lax.fori_loop(0, OWN // FACE, scatter_own, 0)
        land_both(back_copies)
        incoming = jnp.concatenate([back[k, 0], back[k, 1]], axis=1)
        added = lax.dot_general(incoming, face_table[...], NT, preferred_element_type=F32)
        current = target[...] + (added if k == 0 else 2.0 * added)
        if k < DEGREE - 1:
            target[...] = current
            rounded[...] = current.astype(BF16)
        else:
            for p in range(PIECES):
                blocks[o, p] = current[:, p * PIECE : (p + 1) * PIECE].astype(BF16)
        leave_both(halo_copies)
        leave_both(back_copies)

    def turn(at):
        return lax.rem(at + BLOCKS, BLOCKS)

    ways = (1, -1)
    far = BLOCKS // 2

    def moves(way, d, p):
        return d < far or (d == far and (p < PIECES // 2) == (way == 0))

    def ring(way, d, p):
        step = ways[way]
        held = blocks.at[turn(o - step * (d - 1)), p]
        return copy(
            held, held, ring_ssem.at[way, d - 1, p], ring_rsem.at[way, d - 1, p],
            orb=turn(o + step),
        )

    sent = []
    for d in range(1, far + 2):
        for p in range(PIECES):
            for way in range(2):
                if d > 1 and moves(way, d - 1, p):
                    ring(way, d - 1, p).wait_recv()
                if d <= far and moves(way, d, p):
                    one = ring(way, d, p)
                    one.start()
                    sent.append(one)

    strip = jnp.zeros((ROWS, ALL), F32)
    for p in range(PIECES):
        strip += lax.dot_general(
            blocks[o, p], blocks[:, p].reshape(ALL, PIECE), NT, preferred_element_type=F32
        )
    halves[0] = strip[:HALF]
    halves[1] = strip[HALF:]

    one = copy(halves.at[1 - core], half_in, core_ssem, core_rsem, slab=other_core)
    one.start()
    one.wait()
    along_x[0] = halves[core] + half_in[...]
    copies = [
        copy(
            along_x.at[0], along_x.at[d], x_ssem.at[d], x_rsem.at[d],
            slab=slab_of(lax.rem(x + d, SIDE), y, core),
        )
        for d in range(1, SIDE)
    ]
    for one in copies:
        one.start()
    for one in copies:
        one.wait()
    along_y[0] = (along_x[0] + along_x[1]) + (along_x[2] + along_x[3])
    copies = [
        copy(
            along_y.at[0], along_y.at[d], y_ssem.at[d], y_rsem.at[d],
            slab=slab_of(x, lax.rem(y + d, SIDE), core),
        )
        for d in range(1, SIDE)
    ]
    for one in copies:
        one.start()
    for one in copies:
        one.wait()
    rows_all[core, o] = (along_y[0] + along_y[1]) + (along_y[2] + along_y[3])

    def pair(k):
        held = rows_all.at[core, k]
        return copy(held, held, pair_ssem.at[k], pair_rsem.at[k], slab=other_core)

    copies = [
        copy(
            rows_all.at[core, o], rows_all.at[core, o], z_ssem.at[d], z_rsem.at[d],
            orb=turn(o + d),
        )
        for d in range(1, BLOCKS)
    ]
    for d in (4, 3, 5, 2, 6, 1, 7):
        copies[d - 1].start()
    pair(o).start()
    for d in (1, 7, 2, 6, 3, 5, 4):
        copies[d - 1].wait_recv()
        pair(turn(o - d)).start()
    for k in range(BLOCKS):
        pair(k).wait()
    for one in copies + sent:
        one.wait_send()

    for k in range(BLOCKS):
        for h in range(2):
            first = k * ROWS + h * HALF
            gram[first : first + HALF, :] = rows_all[h, k]
    invert_factor(gram, inverse)

    weights = inverse[o] * math.sqrt(OWN * SLABS)
    upper = weights.astype(BF16)
    lower = (weights - upper.astype(F32)).astype(BF16)
    weights = jnp.concatenate([upper, lower], axis=0)
    for p in range(PIECES):
        both = jnp.dot(weights, blocks[:, p].reshape(ALL, PIECE), preferred_element_type=F32)
        out[:, p * PIECE : (p + 1) * PIECE] = both[:ROWS] + both[ROWS:]


def per_device(orbitals, cell_matrices, connectivity, face_lower, face_upper):
    faces = jnp.concatenate([face_lower, face_upper], axis=0)[None, :]
    vmem = pl.BlockSpec(memory_space=pltpu.VMEM)
    dma = pltpu.SemaphoreType.DMA
    return pl.pallas_call(
        kernel,
        out_shape=jax.ShapeDtypeStruct((ROWS, OWN), F32),
        in_specs=[vmem, vmem, vmem, pl.BlockSpec(memory_space=pl.ANY)],
        out_specs=vmem,
        scratch_shapes=[
            pltpu.VMEM((CELLS, OWN + 2 * FACE, LOCAL), BF16),
            pltpu.VMEM((OWN, 2 * FACE), BF16),
            pltpu.VMEM((CELLS, LOCAL, LOCAL), BF16),
            pltpu.VMEM((ROWS, OWN), F32),
            pltpu.VMEM((ROWS, OWN), F32),
            pltpu.VMEM((ROWS, OWN), BF16),
            pltpu.VMEM((CELLS, ROWS, LOCAL), BF16),
            pltpu.VMEM((CELLS, ROWS, LOCAL), BF16),
            pltpu.VMEM((DEGREE, 2, ROWS, FACE), BF16),
            pltpu.VMEM((DEGREE, 2, ROWS, FACE), BF16),
            pltpu.VMEM((DEGREE, 2, ROWS, FACE), BF16),
            pltpu.VMEM((DEGREE, 2, ROWS, FACE), BF16),
            pltpu.VMEM((BLOCKS, PIECES, ROWS, PIECE), BF16),
            pltpu.VMEM((2, HALF, ALL), F32),
            pltpu.VMEM((HALF, ALL), F32),
            pltpu.VMEM((SIDE, HALF, ALL), F32),
            pltpu.VMEM((SIDE, HALF, ALL), F32),
            pltpu.VMEM((2, BLOCKS, HALF, ALL), F32),
            pltpu.VMEM((ALL, ALL), F32),
            pltpu.VMEM((BLOCKS, ROWS, ALL), F32),
            dma,
            dma((DEGREE, 2)), dma((DEGREE, 2)), dma((DEGREE, 2)), dma((DEGREE, 2)),
            dma((2, BLOCKS // 2, PIECES)), dma((2, BLOCKS // 2, PIECES)),
            dma, dma,
            dma((SIDE,)), dma((SIDE,)), dma((SIDE,)), dma((SIDE,)),
            dma((BLOCKS,)), dma((BLOCKS,)), dma((BLOCKS,)), dma((BLOCKS,)),
        ],
        compiler_params=pltpu.CompilerParams(collective_id=0, has_side_effects=True),
        name="filter_and_orthonormalize",
    )(orbitals, connectivity, faces, cell_matrices)


def solution(mesh):
    in_specs = (P("orb", "slab"), P("slab", None, None), P("slab", None), P("slab"), P("slab"))
    return jax.shard_map(
        per_device, mesh=mesh, in_specs=in_specs, out_specs=P("orb", "slab"), check_vma=False
    )
```

```python
import functools
import math

import jax
import jax.numpy as jnp
from jax import lax
from jax.experimental import pallas as pl
from jax.experimental.pallas import tpu as pltpu
from jax.sharding import PartitionSpec as P

MESH = pl.DeviceIdType.MESH
F32, BF16 = jnp.float32, jnp.bfloat16
NT = (((1,), (1,)), ((), ()))
TN = (((0,), (0,)), ((), ()))

DEGREE = 4
CELLS = 8
LOCAL = 512
ROWS = 32
PACK = 16
SUB = 8
LANES = 128
OWN = 2048
FACE = 256
EXT_TILES = 20
BLOCKS = 8
SLABS = 32
SIDE = 4
PIECES = 4
PIECE = OWN // PIECES
HALF = ROWS // 2
ALL = ROWS * BLOCKS


def pick(tile, index):
    numbers = lax.GatherDimensionNumbers(
        offset_dims=(), collapsed_slice_dims=(1,), start_index_map=(1,),
        operand_batching_dims=(0,), start_indices_batching_dims=(0,),
    )
    return lax.gather(
        tile, index[..., None], numbers, (1, 1), mode=lax.GatherScatterMode.PROMISE_IN_BOUNDS
    )


def pick_among(tiles, lane_at, tile_at, start):
    for number, tile in tiles:
        start = jnp.where(tile_at == number, pick(tile, lane_at), start)
    return start


def spread(row):
    return jnp.broadcast_to(row, (PACK, LANES)).astype(jnp.int16)


def split_tables(wanted, table):
    for j in range(LOCAL // LANES):
        part = wanted[:, j * LANES : (j + 1) * LANES]
        table[j, 0] = spread(lax.rem(part, LANES))
        table[j, 1] = spread(part // LANES)


def inverse_tables(wanted, tiles, table):
    number = lax.broadcasted_iota(jnp.int32, (1, LOCAL), 1)
    at_tile = lax.broadcasted_iota(jnp.int32, (ROWS, LOCAL), 0) == wanted // LANES
    lanes = jnp.where(at_tile, lax.rem(number, LANES).astype(F32), 0.0)
    numbers = jnp.where(at_tile, (number // LANES + 1).astype(F32), 0.0)
    at_lane = lax.broadcasted_iota(jnp.int32, (LANES, LOCAL), 0) == lax.rem(wanted, LANES)
    found = lax.dot_general(
        jnp.concatenate([lanes, numbers], axis=0).astype(BF16),
        jnp.where(at_lane, 1.0, 0.0).astype(BF16),
        NT, preferred_element_type=F32,
    ).astype(jnp.int32)
    for t in range(tiles):
        table[t, 0] = spread(found[t : t + 1])
        table[t, 1] = spread(found[ROWS + t : ROWS + t + 1] - 1)


def split3(x):
    high = x.astype(BF16)
    rest = x - high.astype(F32)
    middle = rest.astype(BF16)
    low = (rest - middle.astype(F32)).astype(BF16)
    return high, middle, low


def invert_factor(gram, inverse):
    groups = ROWS // SUB
    sub = lax.broadcasted_iota(jnp.int32, (SUB, LANES), 0)
    lane = lax.broadcasted_iota(jnp.int32, (SUB, LANES), 1)
    wide = lax.broadcasted_iota(jnp.int32, (ROWS, ALL), 1)
    zero = jnp.zeros((SUB, LANES), F32)

    def row_of(tile, j):
        return jnp.broadcast_to(tile[j : j + 1, :], (SUB, LANES))

    def column_of(tile, j):
        return jnp.broadcast_to(tile[:, j : j + 1], (SUB, LANES))

    strip = gram[:ROWS, :]
    for b in range(BLOCKS):
        low, high = b * ROWS, (b + 1) * ROWS
        home, shift = low // LANES, low % LANES
        tiles = [
            [strip[g * SUB : (g + 1) * SUB, h * LANES : (h + 1) * LANES] for h in range(2)]
            + [jnp.where(lane - shift == sub + g * SUB, 1.0, 0.0)]
            for g in range(groups)
        ]
        scales = []
        for q in range(groups):
            columns = [
                [column_of(tiles[g][home], shift + q * SUB + k) for g in range(q, groups)]
                for k in range(SUB)
            ]
            pivots = zero
            for j in range(SUB):
                pivot = row_of(columns[j][0], j)
                pivots = jnp.where(sub == j, pivot, pivots)
                inv = 1.0 / pivot
                factors = [jnp.where(sub > j, columns[j][0], 0.0)] + columns[j][1:]
                for k in range(j + 1, SUB):
                    scaled = row_of(columns[k][0], j) * inv
                    columns[k] = [c - m * scaled for c, m in zip(columns[k], factors)]
                rows = [row_of(t, j) * inv for t in tiles[q]]
                for g in range(q, groups):
                    tiles[g] = [t - factors[g - q] * r for t, r in zip(tiles[g], rows)]
            scales.append(lax.rsqrt(pivots))
        tiles = [[t * scales[g] for t in tiles[g]] for g in range(groups)]
        parts = []
        for h in range(2):
            part = jnp.concatenate([tiles[g][h] for g in range(groups)], axis=0)
            if h == home:
                unit = jnp.concatenate([tiles[g][2] for g in range(groups)], axis=0)
                at = lax.broadcasted_iota(jnp.int32, (ROWS, LANES), 1)
                part = jnp.where((at >= shift) & (at < shift + ROWS), unit, part)
            parts.append(part)
        strip = jnp.concatenate(parts, axis=1)
        inverse[b] = jnp.where(wide < high, strip, 0.0)
        if b < BLOCKS - 1:
            h0, m0, l0 = split3(strip)
            right = jnp.concatenate([h0, m0, h0, m0, l0, h0], axis=0)
            left = jnp.concatenate([h0, h0, m0, m0, h0, l0], axis=0)[:, high:]

            def updated(rest, first, last):
                update = lax.dot_general(
                    left[:, first - high : last - high], right, TN, preferred_element_type=F32
                )
                at = lax.broadcasted_iota(jnp.int32, rest.shape, 1)
                return jnp.where((at >= low) & (at < high), 0.0, rest) - update

            strip = updated(gram[high : high + ROWS, :], high, high + ROWS)
            if b < BLOCKS - 2:
                gram[high + ROWS :, :] = updated(gram[high + ROWS :, :], high + ROWS, ALL)


def kernel(
    orbitals, connectivity, faces, matrices_hbm, out,
    gather_at, scatter_at, face_from, face_to, matrices, field_a, field_b, rounded, pieces, terms,
    halo, halo_out, back, back_out, blocks, halves, half_in, along_x, along_y, rows_all,
    gram, inverse,
    load_sem, halo_ssem, halo_rsem, back_ssem, back_rsem, ring_ssem, ring_rsem,
    core_ssem, core_rsem, x_ssem, x_rsem, y_ssem, y_rsem, z_ssem, z_rsem, pair_ssem, pair_rsem,
):
    s, o = lax.axis_index("slab"), lax.axis_index("orb")
    core, y, x = lax.rem(s, 2), lax.rem(s // 2, SIDE), s // (2 * SIDE)
    other_core = s + 1 - 2 * core

    load = pltpu.make_async_copy(matrices_hbm, matrices, load_sem)
    load.start()

    def slab_of(x_at, y_at, core_at):
        return (x_at * SIDE + y_at) * 2 + core_at

    def copy(source, target, ssem, rsem, **device):
        return pltpu.make_async_remote_copy(
            src_ref=source, dst_ref=target, send_sem=ssem, recv_sem=rsem,
            device_id=device, device_id_type=MESH,
        )

    up, down = lax.rem(s + 1, SLABS), lax.rem(s + SLABS - 1, SLABS)
    has = (s > 0, s < SLABS - 1)
    neighbour = (down, up)

    halo[...] = jnp.zeros_like(halo)
    back[...] = jnp.zeros_like(back)

    barrier = pltpu.get_barrier_semaphore()
    for d in range(1, BLOCKS):
        pl.semaphore_signal(
            barrier, inc=1, device_id={"orb": lax.rem(o + d, BLOCKS)}, device_id_type=MESH
        )
    for d in range(1, SIDE):
        for there in (
            slab_of(lax.rem(x + d, SIDE), y, core),
            slab_of(x, lax.rem(y + d, SIDE), core),
        ):
            pl.semaphore_signal(barrier, inc=1, device_id={"slab": there}, device_id_type=MESH)
    for there in neighbour:
        pl.semaphore_signal(barrier, inc=1, device_id={"slab": there}, device_id_type=MESH)

    field_a[...] = orbitals[...]
    rounded[...] = orbitals[...].astype(BF16)
    split_tables(faces[...], face_from)
    inverse_tables(faces[...], OWN // LANES, face_to)

    pl.semaphore_wait(barrier, BLOCKS - 1 + 2 * (SIDE - 1) + 2)

    def exchange(k, sent, received, ssem, rsem):
        return [
            copy(
                sent.at[k, side], received.at[k, 1 - side],
                ssem.at[k, side], rsem.at[k, 1 - side], slab=neighbour[side],
            )
            for side in range(2)
        ]

    def start_both(copies):
        for side in range(2):
            pl.when(has[side])(copies[side].start)

    def land_both(copies):
        for side in range(2):
            pl.when(has[side])(copies[1 - side].wait_recv)

    def leave_both(copies):
        for side in range(2):
            pl.when(has[side])(copies[side].wait_send)

    groups = [slice(g * PACK, (g + 1) * PACK) for g in range(ROWS // PACK)]
    local_tiles, side_tiles, own_tiles = LOCAL // LANES, FACE // LANES, OWN // LANES
    nothing = jnp.zeros((PACK, LANES), BF16)

    def span(t, width=LANES):
        return slice(t * width, (t + 1) * width)

    def side_of(buffer, k, t, g):
        return buffer[k, t // side_tiles, groups[g], span(t % side_tiles)]

    def send_faces(k):
        for j in range(2 * side_tiles):
            for rows in groups:
                halo_out[k, j // side_tiles, rows, span(j % side_tiles)] = pick_among(
                    [(t, rounded[rows, span(t)]) for t in range(own_tiles)],
                    face_from[j, 0], face_from[j, 1], nothing,
                )
        copies = exchange(k, halo_out, halo, halo_ssem, halo_rsem)
        start_both(copies)
        return copies

    def gathered(t, g):
        total = jnp.zeros((PACK, LANES), F32)
        for c in range(CELLS):
            total += pick_among(
                [(h, terms[c, groups[g], span(h)]) for h in range(local_tiles)],
                scatter_at[c, t, 0], scatter_at[c, t, 1], nothing,
            ).astype(F32)
        return total

    fields = [field_a, field_b]
    for k in range(DEGREE):
        halo_copies = send_faces(k)
        if k == 0:

            def tables(c, _):
                wanted = connectivity[pl.ds(c, 1), :]
                split_tables(wanted, gather_at.at[c])
                inverse_tables(wanted, EXT_TILES, scatter_at.at[c])
                return 0

            lax.fori_loop(0, CELLS, tables, 0)

        def gather_own(i, _):
            for c in (2 * i, 2 * i + 1):
                for j in range(local_tiles):
                    for rows in groups:
                        pieces[c, rows, span(j)] = pick_among(
                            [(t + side_tiles, rounded[rows, span(t)]) for t in range(own_tiles)],
                            gather_at[c, j, 0], gather_at[c, j, 1], nothing,
                        )
            return 0

        lax.fori_loop(0, CELLS // 2, gather_own, 0)
        if k == 0:
            load.wait()
        land_both(halo_copies)

        def cell(i, _):
            for c in (2 * i, 2 * i + 1):
                for j in range(local_tiles):
                    for g, rows in enumerate(groups):
                        pieces[c, rows, span(j)] = pick_among(
                            [
                                (t if t < side_tiles else t + own_tiles, side_of(halo, k, t, g))
                                for t in range(2 * side_tiles)
                            ],
                            gather_at[c, j, 0], gather_at[c, j, 1], pieces[c, rows, span(j)],
                        )
                terms[c] = jnp.dot(
                    pieces[c], matrices[c], preferred_element_type=F32
                ).astype(BF16)
            return 0

        lax.fori_loop(0, CELLS // 2, cell, 0)
        for t in range(2 * side_tiles):
            for g, rows in enumerate(groups):
                back_out[k, t // side_tiles, rows, span(t % side_tiles)] = gathered(
                    t if t < side_tiles else t + own_tiles, g
                ).astype(BF16)
        back_copies = exchange(k, back_out, back, back_ssem, back_rsem)
        start_both(back_copies)

        target = fields[(k + 1) % 2]

        def scatter_own(i, _):
            for t in (2 * i, 2 * i + 1):
                columns = pl.ds(pl.multiple_of(t * LANES, LANES), LANES)
                for g, rows in enumerate(groups):
                    total = gathered(t + side_tiles, g)
                    if k > 0:
                        total = 2.0 * total - target[rows, columns]
                    target[rows, columns] = total
            return 0

        lax.fori_loop(0, own_tiles // 2, scatter_own, 0)
        land_both(back_copies)
        for t in range(own_tiles):
            for g, rows in enumerate(groups):
                added = pick_among(
                    [(h, side_of(back, k, h, g)) for h in range(2 * side_tiles)],
                    face_to[t, 0], face_to[t, 1], nothing,
                ).astype(F32)
                current = target[rows, span(t)] + (added if k == 0 else 2.0 * added)
                if k < DEGREE - 1:
                    target[rows, span(t)] = current
                    rounded[rows, span(t)] = current.astype(BF16)
                else:
                    p, q = divmod(t, PIECE // LANES)
                    blocks[o, p, rows, span(q)] = current.astype(BF16)
        leave_both(halo_copies)
        leave_both(back_copies)

    def turn(at):
        return lax.rem(at + BLOCKS, BLOCKS)

    ways = (1, -1)
    far = BLOCKS // 2

    def moves(way, d, p):
        return d < far or (d == far and (p < PIECES // 2) == (way == 0))

    def ring(way, d, p):
        step = ways[way]
        held = blocks.at[turn(o - step * (d - 1)), p]
        return copy(
            held, held, ring_ssem.at[way, d - 1, p], ring_rsem.at[way, d - 1, p],
            orb=turn(o + step),
        )

    sent = []
    for d in range(1, far + 2):
        for p in range(PIECES):
            for way in range(2):
                if d > 1 and moves(way, d - 1, p):
                    ring(way, d - 1, p).wait_recv()
                if d <= far and moves(way, d, p):
                    one = ring(way, d, p)
                    one.start()
                    sent.append(one)

    strip = jnp.zeros((ROWS, ALL), F32)
    for p in range(PIECES):
        strip += lax.dot_general(
            blocks[o, p], blocks[:, p].reshape(ALL, PIECE), NT, preferred_element_type=F32
        )
    halves[0] = strip[:HALF]
    halves[1] = strip[HALF:]

    one = copy(halves.at[1 - core], half_in, core_ssem, core_rsem, slab=other_core)
    one.start()
    one.wait()
    along_x[0] = halves[core] + half_in[...]
    copies = [
        copy(
            along_x.at[0], along_x.at[d], x_ssem.at[d], x_rsem.at[d],
            slab=slab_of(lax.rem(x + d, SIDE), y, core),
        )
        for d in range(1, SIDE)
    ]
    for one in copies:
        one.start()
    for one in copies:
        one.wait()
    along_y[0] = (along_x[0] + along_x[1]) + (along_x[2] + along_x[3])
    copies = [
        copy(
            along_y.at[0], along_y.at[d], y_ssem.at[d], y_rsem.at[d],
            slab=slab_of(x, lax.rem(y + d, SIDE), core),
        )
        for d in range(1, SIDE)
    ]
    for one in copies:
        one.start()
    for one in copies:
        one.wait()
    rows_all[core, o] = (along_y[0] + along_y[1]) + (along_y[2] + along_y[3])

    def pair(k):
        held = rows_all.at[core, k]
        return copy(held, held, pair_ssem.at[k], pair_rsem.at[k], slab=other_core)

    copies = [
        copy(
            rows_all.at[core, o], rows_all.at[core, o], z_ssem.at[d], z_rsem.at[d],
            orb=turn(o + d),
        )
        for d in range(1, BLOCKS)
    ]
    for d in (4, 3, 5, 2, 6, 1, 7):
        copies[d - 1].start()
    pair(o).start()
    for d in (1, 7, 2, 6, 3, 5, 4):
        copies[d - 1].wait_recv()
        pair(turn(o - d)).start()
    for k in range(BLOCKS):
        pair(k).wait()
    for one in copies + sent:
        one.wait_send()

    for k in range(BLOCKS):
        for h in range(2):
            first = k * ROWS + h * HALF
            gram[first : first + HALF, :] = rows_all[h, k]
    invert_factor(gram, inverse)

    weights = inverse[o] * math.sqrt(OWN * SLABS)
    upper = weights.astype(BF16)
    lower = (weights - upper.astype(F32)).astype(BF16)
    weights = jnp.concatenate([upper, lower], axis=0)
    for p in range(PIECES):
        both = jnp.dot(weights, blocks[:, p].reshape(ALL, PIECE), preferred_element_type=F32)
        out[:, p * PIECE : (p + 1) * PIECE] = both[:ROWS] + both[ROWS:]


def per_device(orbitals, cell_matrices, connectivity, face_lower, face_upper):
    faces = jnp.concatenate([face_lower, face_upper], axis=0)[None, :]
    vmem = pl.BlockSpec(memory_space=pltpu.VMEM)
    dma = pltpu.SemaphoreType.DMA
    return pl.pallas_call(
        kernel,
        out_shape=jax.ShapeDtypeStruct((ROWS, OWN), F32),
        in_specs=[vmem, vmem, vmem, pl.BlockSpec(memory_space=pl.ANY)],
        out_specs=vmem,
        scratch_shapes=[
            pltpu.VMEM((CELLS, LOCAL // LANES, 2, PACK, LANES), jnp.int16),
            pltpu.VMEM((CELLS, EXT_TILES, 2, PACK, LANES), jnp.int16),
            pltpu.VMEM((LOCAL // LANES, 2, PACK, LANES), jnp.int16),
            pltpu.VMEM((OWN // LANES, 2, PACK, LANES), jnp.int16),
            pltpu.VMEM((CELLS, LOCAL, LOCAL), BF16),
            pltpu.VMEM((ROWS, OWN), F32),
            pltpu.VMEM((ROWS, OWN), F32),
            pltpu.VMEM((ROWS, OWN), BF16),
            pltpu.VMEM((CELLS, ROWS, LOCAL), BF16),
            pltpu.VMEM((CELLS, ROWS, LOCAL), BF16),
            pltpu.VMEM((DEGREE, 2, ROWS, FACE), BF16),
            pltpu.VMEM((DEGREE, 2, ROWS, FACE), BF16),
            pltpu.VMEM((DEGREE, 2, ROWS, FACE), BF16),
            pltpu.VMEM((DEGREE, 2, ROWS, FACE), BF16),
            pltpu.VMEM((BLOCKS, PIECES, ROWS, PIECE), BF16),
            pltpu.VMEM((2, HALF, ALL), F32),
            pltpu.VMEM((HALF, ALL), F32),
            pltpu.VMEM((SIDE, HALF, ALL), F32),
            pltpu.VMEM((SIDE, HALF, ALL), F32),
            pltpu.VMEM((2, BLOCKS, HALF, ALL), F32),
            pltpu.VMEM((ALL, ALL), F32),
            pltpu.VMEM((BLOCKS, ROWS, ALL), F32),
            dma,
            dma((DEGREE, 2)), dma((DEGREE, 2)), dma((DEGREE, 2)), dma((DEGREE, 2)),
            dma((2, BLOCKS // 2, PIECES)), dma((2, BLOCKS // 2, PIECES)),
            dma, dma,
            dma((SIDE,)), dma((SIDE,)), dma((SIDE,)), dma((SIDE,)),
            dma((BLOCKS,)), dma((BLOCKS,)), dma((BLOCKS,)), dma((BLOCKS,)),
        ],
        compiler_params=pltpu.CompilerParams(collective_id=0, has_side_effects=True),
        name="filter_and_orthonormalize",
    )(orbitals, connectivity, faces, cell_matrices)


def solution(mesh):
    in_specs = (P("orb", "slab"), P("slab", None, None), P("slab", None), P("slab"), P("slab"))
    return jax.shard_map(
        per_device, mesh=mesh, in_specs=in_specs, out_specs=P("orb", "slab"), check_vma=False
    )
```

```python
import functools
import math

import jax
import jax.numpy as jnp
from jax import lax
from jax.experimental import pallas as pl
from jax.experimental.pallas import tpu as pltpu
from jax.sharding import PartitionSpec as P

MESH = pl.DeviceIdType.MESH
F32, BF16 = jnp.float32, jnp.bfloat16
NT = (((1,), (1,)), ((), ()))
TN = (((0,), (0,)), ((), ()))

DEGREE = 4
CELLS = 8
LOCAL = 512
ROWS = 32
PACK = 16
SUB = 8
LANES = 128
OWN = 2048
FACE = 256
OWN_TILES = OWN // LANES
BORDER_TILES = 8
BORDER = BORDER_TILES * LANES
TILES = OWN_TILES + BORDER_TILES
BLOCKS = 8
SLABS = 32
SIDE = 4
STEP_TILES = 4
PIECES = 4
PIECE = OWN // PIECES
HALF = ROWS // 2
ALL = ROWS * BLOCKS


def pick(tile, index):
    numbers = lax.GatherDimensionNumbers(
        offset_dims=(), collapsed_slice_dims=(1,), start_index_map=(1,),
        operand_batching_dims=(0,), start_indices_batching_dims=(0,),
    )
    return lax.gather(
        tile, index[..., None], numbers, (1, 1), mode=lax.GatherScatterMode.PROMISE_IN_BOUNDS
    )


def pick_among(tiles, lane_at, tile_at, start):
    for number, tile in tiles:
        start = jnp.where(tile_at == number, pick(tile, lane_at), start)
    return start


def spread(row):
    return jnp.broadcast_to(row, (PACK, LANES)).astype(jnp.int16)


def lane_of(position):
    return jnp.bitwise_and(position, LANES - 1)


def tile_of(position):
    return lax.shift_right_arithmetic(position, 7)


def split_tables(wanted, table):
    for j in range(LOCAL // LANES):
        part = wanted[:, j * LANES : (j + 1) * LANES]
        table[j, 0] = spread(lane_of(part))
        table[j, 1] = spread(tile_of(part))


def find(wanted):
    number = lax.broadcasted_iota(jnp.int32, (1, LOCAL), 1)
    at_tile = lax.broadcasted_iota(jnp.int32, (ROWS, LOCAL), 0) == tile_of(wanted)
    lanes = jnp.where(at_tile, lane_of(number).astype(F32), 0.0)
    numbers = jnp.where(at_tile, (tile_of(number) + 1).astype(F32), 0.0)
    at_lane = lax.broadcasted_iota(jnp.int32, (LANES, LOCAL), 0) == lane_of(wanted)
    return lax.dot_general(
        jnp.concatenate([lanes, numbers], axis=0).astype(BF16),
        jnp.where(at_lane, 1.0, 0.0).astype(BF16),
        NT, preferred_element_type=F32,
    ).astype(jnp.int32)


def inverse_tables(found, tiles, table):
    for t in range(tiles):
        table[t, 0] = spread(found[t : t + 1])
        table[t, 1] = spread(found[ROWS + t : ROWS + t + 1] - 1)


def split3(x):
    high = x.astype(BF16)
    rest = x - high.astype(F32)
    middle = rest.astype(BF16)
    low = (rest - middle.astype(F32)).astype(BF16)
    return high, middle, low


def invert_factor(gram, inverse):
    groups = ROWS // SUB
    sub = lax.broadcasted_iota(jnp.int32, (SUB, LANES), 0)
    lane = lax.broadcasted_iota(jnp.int32, (SUB, LANES), 1)
    wide = lax.broadcasted_iota(jnp.int32, (ROWS, ALL), 1)
    zero = jnp.zeros((SUB, LANES), F32)

    def row_of(tile, j):
        return jnp.broadcast_to(tile[j : j + 1, :], (SUB, LANES))

    def column_of(tile, j):
        return jnp.broadcast_to(tile[:, j : j + 1], (SUB, LANES))

    strip = gram[:ROWS, :]
    for b in range(BLOCKS):
        low, high = b * ROWS, (b + 1) * ROWS
        home, shift = low // LANES, low % LANES
        tiles = [
            [strip[g * SUB : (g + 1) * SUB, h * LANES : (h + 1) * LANES] for h in range(2)]
            + [jnp.where(lane - shift == sub + g * SUB, 1.0, 0.0)]
            for g in range(groups)
        ]
        scales = []
        for q in range(groups):
            columns = [
                [column_of(tiles[g][home], shift + q * SUB + k) for g in range(q, groups)]
                for k in range(SUB)
            ]
            pivots = zero
            for j in range(SUB):
                pivot = row_of(columns[j][0], j)
                pivots = jnp.where(sub == j, pivot, pivots)
                inv = 1.0 / pivot
                factors = [jnp.where(sub > j, columns[j][0], 0.0)] + columns[j][1:]
                for k in range(j + 1, SUB):
                    scaled = row_of(columns[k][0], j) * inv
                    columns[k] = [c - m * scaled for c, m in zip(columns[k], factors)]
                rows = [row_of(t, j) * inv for t in tiles[q]]
                for g in range(q, groups):
                    tiles[g] = [t - factors[g - q] * r for t, r in zip(tiles[g], rows)]
            scales.append(lax.rsqrt(pivots))
        tiles = [[t * scales[g] for t in tiles[g]] for g in range(groups)]
        parts = []
        for h in range(2):
            part = jnp.concatenate([tiles[g][h] for g in range(groups)], axis=0)
            if h == home:
                unit = jnp.concatenate([tiles[g][2] for g in range(groups)], axis=0)
                at = lax.broadcasted_iota(jnp.int32, (ROWS, LANES), 1)
                part = jnp.where((at >= shift) & (at < shift + ROWS), unit, part)
            parts.append(part)
        strip = jnp.concatenate(parts, axis=1)
        inverse[b] = jnp.where(wide < high, strip, 0.0)
        if b < BLOCKS - 1:
            h0, m0, l0 = split3(strip)
            right = jnp.concatenate([h0, m0, h0, m0, l0, h0], axis=0)
            left = jnp.concatenate([h0, h0, m0, m0, h0, l0], axis=0)[:, high:]

            def updated(rest, first, last):
                update = lax.dot_general(
                    left[:, first - high : last - high], right, TN, preferred_element_type=F32
                )
                at = lax.broadcasted_iota(jnp.int32, rest.shape, 1)
                return jnp.where((at >= low) & (at < high), 0.0, rest) - update

            strip = updated(gram[high : high + ROWS, :], high, high + ROWS)
            if b < BLOCKS - 2:
                gram[high + ROWS :, :] = updated(gram[high + ROWS :, :], high + ROWS, ALL)


def kernel(
    orbitals, connectivity, lower, upper, matrices_hbm, out,
    places, gather_at, scatter_at, face_to, matrices, field_a, field_b, border_a, border_b,
    part, rounded, rounded_border, pieces, terms,
    first_out, first_in, shared_out, shared_in,
    blocks, halves, half_in, along_x, along_y, rows_all, gram, inverse,
    load_sem, first_ssem, first_rsem, shared_ssem, shared_rsem, ring_ssem, ring_rsem,
    core_ssem, core_rsem, x_ssem, x_rsem, y_ssem, y_rsem, z_ssem, z_rsem, pair_ssem, pair_rsem,
):
    s, o = lax.axis_index("slab"), lax.axis_index("orb")
    core, y, x = lax.rem(s, 2), lax.rem(s // 2, SIDE), s // (2 * SIDE)
    other_core = s + 1 - 2 * core

    def slab_of(x_at, y_at, core_at):
        return (x_at * SIDE + y_at) * 2 + core_at

    def copy(source, target, ssem, rsem, **device):
        return pltpu.make_async_remote_copy(
            src_ref=source, dst_ref=target, send_sem=ssem, recv_sem=rsem,
            device_id=device, device_id_type=MESH,
        )

    up, down = lax.rem(s + 1, SLABS), lax.rem(s + SLABS - 1, SLABS)
    has = (s > 0, s < SLABS - 1)
    neighbour = (down, up)

    first_in[...] = jnp.zeros_like(first_in)
    shared_in[...] = jnp.zeros_like(shared_in)

    barrier = pltpu.get_barrier_semaphore()
    for d in range(1, BLOCKS):
        pl.semaphore_signal(
            barrier, inc=1, device_id={"orb": lax.rem(o + d, BLOCKS)}, device_id_type=MESH
        )
    for d in range(1, SIDE):
        for there in (
            slab_of(lax.rem(x + d, SIDE), y, core),
            slab_of(x, lax.rem(y + d, SIDE), core),
        ):
            pl.semaphore_signal(barrier, inc=1, device_id={"slab": there}, device_id_type=MESH)
    for there in neighbour:
        pl.semaphore_signal(barrier, inc=1, device_id={"slab": there}, device_id_type=MESH)

    load = pltpu.make_async_copy(matrices_hbm, matrices, load_sem)
    load.start()

    groups = [slice(g * PACK, (g + 1) * PACK) for g in range(ROWS // PACK)]
    local_tiles, side_tiles = LOCAL // LANES, FACE // LANES

    def span(t, width=LANES):
        return slice(t * width, (t + 1) * width)

    faces = jnp.concatenate([lower[...], upper[...]], axis=1)
    for j in range(2 * side_tiles):
        lane_at = jnp.broadcast_to(lane_of(faces[:, span(j)]), (SUB, LANES))
        tile_at = jnp.broadcast_to(tile_of(faces[:, span(j)]), (SUB, LANES))
        for g in range(ROWS // SUB):
            rows = span(g, SUB)
            values = pick_among(
                [(t, orbitals[rows, span(t)]) for t in range(OWN_TILES)],
                lane_at, tile_at, jnp.zeros((SUB, LANES), F32),
            )
            border_a[rows, span(j)] = values
            first_out[j // side_tiles, rows, span(j % side_tiles)] = values
    field_a[...] = orbitals[...]
    rounded[...] = orbitals[...].astype(BF16)

    found = find(faces)
    inverse_tables(found, OWN_TILES, face_to)
    for j in range(local_tiles):
        wanted = connectivity[:, span(j)]
        own = wanted - FACE
        face = jnp.full((CELLS, LANES), -1, jnp.int32)
        for t in range(OWN_TILES):
            row = found[t : t + 1] + LANES * (found[ROWS + t : ROWS + t + 1] - 1)
            face = pick_among(
                [(t, jnp.broadcast_to(row, (CELLS, LANES)))], lane_of(own), tile_of(own), face
            )
        place = jnp.where(face >= 0, face + OWN, own)
        place = jnp.where(wanted < FACE, wanted + (OWN + 2 * FACE), place)
        places[:, span(j)] = jnp.where(wanted >= OWN + FACE, wanted + 2 * FACE, place)

    def tables(c, _):
        wanted = places[pl.ds(c, 1), :]
        split_tables(wanted, gather_at.at[c])
        inverse_tables(find(wanted), TILES, scatter_at.at[c])
        return 0

    lax.fori_loop(0, CELLS, tables, 0)

    pl.semaphore_wait(barrier, BLOCKS - 1 + 2 * (SIDE - 1) + 2)

    def exchange(sent, received, ssem, rsem, *at):
        return [
            copy(
                sent.at[(*at, side)], received.at[(*at, 1 - side)],
                ssem.at[(*at, side)], rsem.at[(*at, 1 - side)], slab=neighbour[side],
            )
            for side in range(2)
        ]

    def start_both(copies):
        for side in range(2):
            pl.when(has[side])(copies[side].start)

    def land_both(copies):
        for side in range(2):
            pl.when(has[side])(copies[1 - side].wait_recv)

    def leave_both(copies):
        for side in range(2):
            pl.when(has[side])(copies[side].wait_send)

    first = exchange(first_out, first_in, first_ssem, first_rsem)
    start_both(first)

    nothing = jnp.zeros((PACK, LANES), BF16)

    def gather_own(i, _):
        for c in (2 * i, 2 * i + 1):
            for j in range(local_tiles):
                for rows in groups:
                    pieces[c, rows, span(j)] = pick_among(
                        [(t, rounded[rows, span(t)]) for t in range(OWN_TILES)],
                        gather_at[c, j, 0], gather_at[c, j, 1], nothing,
                    )
        return 0

    def multiply(i, _):
        for c in (2 * i, 2 * i + 1):
            for j in range(local_tiles):
                for rows in groups:
                    pieces[c, rows, span(j)] = pick_among(
                        [
                            (OWN_TILES + t, rounded_border[rows, span(t)])
                            for t in range(BORDER_TILES)
                        ],
                        gather_at[c, j, 0], gather_at[c, j, 1], pieces[c, rows, span(j)],
                    )
            terms[c] = jnp.dot(pieces[c], matrices[c], preferred_element_type=F32).astype(BF16)
        return 0

    def gathered(t, g):
        total = jnp.zeros((PACK, LANES), F32)
        for c in range(CELLS):
            total += pick_among(
                [(h, terms[c, groups[g], span(h)]) for h in range(local_tiles)],
                scatter_at[c, t, 0], scatter_at[c, t, 1], nothing,
            ).astype(F32)
        return total

    def scatter_border(i, _):
        for t in range(STEP_TILES):
            t = STEP_TILES * i + t
            columns = pl.ds(pl.multiple_of(t * LANES, LANES), LANES)
            for g, rows in enumerate(groups):
                part[rows, columns] = gathered(OWN_TILES + t, g)
        return 0

    lax.fori_loop(0, CELLS // 2, gather_own, 0)
    load.wait()
    land_both(first)
    for side in range(2):
        border_a[:, span(2 + side, FACE)] = first_in[side]
    rounded_border[...] = border_a[...].astype(BF16)
    leave_both(first)

    fields, borders = [field_a, field_b], [border_a, border_b]
    for k in range(DEGREE):
        lax.fori_loop(0, CELLS // 2, multiply, 0)
        lax.fori_loop(0, BORDER_TILES // STEP_TILES, scatter_border, 0)
        for side in range(2):
            shared_out[k, side, 0] = part[:, span(2 + side, FACE)].astype(BF16)
            shared_out[k, side, 1] = part[:, span(side, FACE)].astype(BF16)
        copies = exchange(shared_out, shared_in, shared_ssem, shared_rsem, k)
        start_both(copies)

        target, target_border = fields[(k + 1) % 2], borders[(k + 1) % 2]

        def scatter_own(i, _):
            for t in range(STEP_TILES):
                t = STEP_TILES * i + t
                columns = pl.ds(pl.multiple_of(t * LANES, LANES), LANES)
                for g, rows in enumerate(groups):
                    total = gathered(t, g)
                    if k > 0:
                        total = 2.0 * total - target[rows, columns]
                    target[rows, columns] = total
                    rounded[rows, columns] = total.astype(BF16)
            return 0

        lax.fori_loop(0, OWN_TILES // STEP_TILES, scatter_own, 0)
        if k < DEGREE - 1:
            lax.fori_loop(0, CELLS // 2, gather_own, 0)
        land_both(copies)
        for side in range(2):
            present = jnp.where(has[side], 1.0, 0.0)
            for kind, columns in enumerate((span(side, FACE), span(2 + side, FACE))):
                total = part[:, columns] + shared_in[k, side, kind].astype(F32)
                if kind == 1:
                    total = total * present
                if k > 0:
                    total = 2.0 * total - target_border[:, columns]
                target_border[:, columns] = total
                rounded_border[:, columns] = total.astype(BF16)
        leave_both(copies)

    for t in range(OWN_TILES):
        p, q = divmod(t, PIECE // LANES)
        for rows in groups:
            blocks[o, p, rows, span(q)] = pick_among(
                [(h, rounded_border[rows, span(h)]) for h in range(2 * side_tiles)],
                face_to[t, 0], face_to[t, 1], rounded[rows, span(t)],
            )

    def turn(at):
        return lax.rem(at + BLOCKS, BLOCKS)

    ways = (1, -1)
    far = BLOCKS // 2

    def moves(way, d, p):
        return d < far or (d == far and (p < PIECES // 2) == (way == 0))

    def ring(way, d, p):
        step = ways[way]
        held = blocks.at[turn(o - step * (d - 1)), p]
        return copy(
            held, held, ring_ssem.at[way, d - 1, p], ring_rsem.at[way, d - 1, p],
            orb=turn(o + step),
        )

    sent = []
    for d in range(1, far + 2):
        for p in range(PIECES):
            for way in range(2):
                if d > 1 and moves(way, d - 1, p):
                    ring(way, d - 1, p).wait_recv()
                if d <= far and moves(way, d, p):
                    one = ring(way, d, p)
                    one.start()
                    sent.append(one)

    strip = jnp.zeros((ROWS, ALL), F32)
    for p in range(PIECES):
        strip += lax.dot_general(
            blocks[o, p], blocks[:, p].reshape(ALL, PIECE), NT, preferred_element_type=F32
        )
    halves[0] = strip[:HALF]
    halves[1] = strip[HALF:]

    one = copy(halves.at[1 - core], half_in, core_ssem, core_rsem, slab=other_core)
    one.start()
    one.wait()
    along_x[0] = halves[core] + half_in[...]
    copies = [
        copy(
            along_x.at[0], along_x.at[d], x_ssem.at[d], x_rsem.at[d],
            slab=slab_of(lax.rem(x + d, SIDE), y, core),
        )
        for d in range(1, SIDE)
    ]
    for one in copies:
        one.start()
    for one in copies:
        one.wait()
    along_y[0] = (along_x[0] + along_x[1]) + (along_x[2] + along_x[3])
    copies = [
        copy(
            along_y.at[0], along_y.at[d], y_ssem.at[d], y_rsem.at[d],
            slab=slab_of(x, lax.rem(y + d, SIDE), core),
        )
        for d in range(1, SIDE)
    ]
    for one in copies:
        one.start()
    for one in copies:
        one.wait()
    rows_all[core, o] = (along_y[0] + along_y[1]) + (along_y[2] + along_y[3])

    def pair(k):
        held = rows_all.at[core, k]
        return copy(held, held, pair_ssem.at[k], pair_rsem.at[k], slab=other_core)

    copies = [
        copy(
            rows_all.at[core, o], rows_all.at[core, o], z_ssem.at[d], z_rsem.at[d],
            orb=turn(o + d),
        )
        for d in range(1, BLOCKS)
    ]
    for d in (4, 3, 5, 2, 6, 1, 7):
        copies[d - 1].start()
    pair(o).start()
    for d in (1, 7, 2, 6, 3, 5, 4):
        copies[d - 1].wait_recv()
        pair(turn(o - d)).start()
    for k in range(BLOCKS):
        pair(k).wait()
    for one in copies + sent:
        one.wait_send()

    for k in range(BLOCKS):
        for h in range(2):
            first = k * ROWS + h * HALF
            gram[first : first + HALF, :] = rows_all[h, k]
    invert_factor(gram, inverse)

    weights = inverse[o] * math.sqrt(OWN * SLABS)
    upper = weights.astype(BF16)
    lower = (weights - upper.astype(F32)).astype(BF16)
    weights = jnp.concatenate([upper, lower], axis=0)
    for p in range(PIECES):
        both = jnp.dot(weights, blocks[:, p].reshape(ALL, PIECE), preferred_element_type=F32)
        out[:, p * PIECE : (p + 1) * PIECE] = both[:ROWS] + both[ROWS:]


def per_device(orbitals, cell_matrices, connectivity, face_lower, face_upper):
    vmem = pl.BlockSpec(memory_space=pltpu.VMEM)
    dma = pltpu.SemaphoreType.DMA
    return pl.pallas_call(
        kernel,
        out_shape=jax.ShapeDtypeStruct((ROWS, OWN), F32),
        in_specs=[vmem, vmem, vmem, vmem, pl.BlockSpec(memory_space=pl.ANY)],
        out_specs=vmem,
        scratch_shapes=[
            pltpu.VMEM((CELLS, LOCAL), jnp.int32),
            pltpu.VMEM((CELLS, LOCAL // LANES, 2, PACK, LANES), jnp.int16),
            pltpu.VMEM((CELLS, TILES, 2, PACK, LANES), jnp.int16),
            pltpu.VMEM((OWN_TILES, 2, PACK, LANES), jnp.int16),
            pltpu.VMEM((CELLS, LOCAL, LOCAL), BF16),
            pltpu.VMEM((ROWS, OWN), F32),
            pltpu.VMEM((ROWS, OWN), F32),
            pltpu.VMEM((ROWS, BORDER), F32),
            pltpu.VMEM((ROWS, BORDER), F32),
            pltpu.VMEM((ROWS, BORDER), F32),
            pltpu.VMEM((ROWS, OWN), BF16),
            pltpu.VMEM((ROWS, BORDER), BF16),
            pltpu.VMEM((CELLS, ROWS, LOCAL), BF16),
            pltpu.VMEM((CELLS, ROWS, LOCAL), BF16),
            pltpu.VMEM((2, ROWS, FACE), F32),
            pltpu.VMEM((2, ROWS, FACE), F32),
            pltpu.VMEM((DEGREE, 2, 2, ROWS, FACE), BF16),
            pltpu.VMEM((DEGREE, 2, 2, ROWS, FACE), BF16),
            pltpu.VMEM((BLOCKS, PIECES, ROWS, PIECE), BF16),
            pltpu.VMEM((2, HALF, ALL), F32),
            pltpu.VMEM((HALF, ALL), F32),
            pltpu.VMEM((SIDE, HALF, ALL), F32),
            pltpu.VMEM((SIDE, HALF, ALL), F32),
            pltpu.VMEM((2, BLOCKS, HALF, ALL), F32),
            pltpu.VMEM((ALL, ALL), F32),
            pltpu.VMEM((BLOCKS, ROWS, ALL), F32),
            dma,
            dma((2,)), dma((2,)), dma((DEGREE, 2)), dma((DEGREE, 2)),
            dma((2, BLOCKS // 2, PIECES)), dma((2, BLOCKS // 2, PIECES)),
            dma, dma,
            dma((SIDE,)), dma((SIDE,)), dma((SIDE,)), dma((SIDE,)),
            dma((BLOCKS,)), dma((BLOCKS,)), dma((BLOCKS,)), dma((BLOCKS,)),
        ],
        compiler_params=pltpu.CompilerParams(collective_id=0, has_side_effects=True),
        name="filter_and_orthonormalize",
    )(orbitals, connectivity, face_lower[None, :], face_upper[None, :], cell_matrices)


def solution(mesh):
    in_specs = (P("orb", "slab"), P("slab", None, None), P("slab", None), P("slab"), P("slab"))
    return jax.shard_map(
        per_device, mesh=mesh, in_specs=in_specs, out_specs=P("orb", "slab"), check_vma=False
    )
```

```python
import functools
import math

import jax
import jax.numpy as jnp
from jax import lax
from jax.experimental import pallas as pl
from jax.experimental.pallas import tpu as pltpu
from jax.sharding import PartitionSpec as P

MESH = pl.DeviceIdType.MESH
F32, BF16 = jnp.float32, jnp.bfloat16
NT = (((1,), (1,)), ((), ()))
TN = (((0,), (0,)), ((), ()))

DEGREE = 4
CELLS = 8
LOCAL = 512
ROWS = 32
PACK = 16
SUB = 8
LANES = 128
OWN = 2048
FACE = 256
OWN_TILES = OWN // LANES
BORDER_TILES = 8
BORDER = BORDER_TILES * LANES
TILES = OWN_TILES + BORDER_TILES
BLOCKS = 8
SLABS = 32
SIDE = 4
STEP_TILES = 4
PIECES = 4
PIECE = OWN // PIECES
HALF = ROWS // 2
SHARED = (ROWS + HALF) // 2
ALL = ROWS * BLOCKS


def pick(tile, index):
    numbers = lax.GatherDimensionNumbers(
        offset_dims=(), collapsed_slice_dims=(1,), start_index_map=(1,),
        operand_batching_dims=(0,), start_indices_batching_dims=(0,),
    )
    return lax.gather(
        tile, index[..., None], numbers, (1, 1), mode=lax.GatherScatterMode.PROMISE_IN_BOUNDS
    )


def pick_among(tiles, lane_at, tile_at, start):
    for number, tile in tiles:
        start = jnp.where(tile_at == number, pick(tile, lane_at), start)
    return start


def spread(row):
    return jnp.broadcast_to(row, (PACK, LANES)).astype(jnp.int16)


def lane_of(position):
    return jnp.bitwise_and(position, LANES - 1)


def tile_of(position):
    return lax.shift_right_arithmetic(position, 7)


def split_tables(wanted, table):
    for j in range(LOCAL // LANES):
        part = wanted[:, j * LANES : (j + 1) * LANES]
        table[j, 0] = spread(lane_of(part))
        table[j, 1] = spread(tile_of(part))


def find(wanted):
    number = lax.broadcasted_iota(jnp.int32, (1, LOCAL), 1)
    at_tile = lax.broadcasted_iota(jnp.int32, (ROWS, LOCAL), 0) == tile_of(wanted)
    lanes = jnp.where(at_tile, lane_of(number).astype(F32), 0.0)
    numbers = jnp.where(at_tile, (tile_of(number) + 1).astype(F32), 0.0)
    at_lane = lax.broadcasted_iota(jnp.int32, (LANES, LOCAL), 0) == lane_of(wanted)
    return lax.dot_general(
        jnp.concatenate([lanes, numbers], axis=0).astype(BF16),
        jnp.where(at_lane, 1.0, 0.0).astype(BF16),
        NT, preferred_element_type=F32,
    ).astype(jnp.int32)


def inverse_tables(found, tiles, table):
    for t in range(tiles):
        table[t, 0] = spread(found[t : t + 1])
        table[t, 1] = spread(found[ROWS + t : ROWS + t + 1] - 1)


def split3(x):
    high = x.astype(BF16)
    rest = x - high.astype(F32)
    middle = rest.astype(BF16)
    low = (rest - middle.astype(F32)).astype(BF16)
    return high, middle, low


def invert_factor(gram, inverse):
    groups = ROWS // SUB
    sub = lax.broadcasted_iota(jnp.int32, (SUB, LANES), 0)
    lane = lax.broadcasted_iota(jnp.int32, (SUB, LANES), 1)
    wide = lax.broadcasted_iota(jnp.int32, (ROWS, ALL), 1)
    zero = jnp.zeros((SUB, LANES), F32)

    def row_of(tile, j):
        return jnp.broadcast_to(tile[j : j + 1, :], (SUB, LANES))

    def column_of(tile, j):
        return jnp.broadcast_to(tile[:, j : j + 1], (SUB, LANES))

    strip = gram[:ROWS, :]
    for b in range(BLOCKS):
        low, high = b * ROWS, (b + 1) * ROWS
        home, shift = low // LANES, low % LANES
        tiles = [
            [strip[g * SUB : (g + 1) * SUB, h * LANES : (h + 1) * LANES] for h in range(2)]
            + [jnp.where(lane - shift == sub + g * SUB, 1.0, 0.0)]
            for g in range(groups)
        ]
        scales = []
        for q in range(groups):
            columns = [
                [column_of(tiles[g][home], shift + q * SUB + k) for g in range(q, groups)]
                for k in range(SUB)
            ]
            pivots = zero
            for j in range(SUB):
                pivot = row_of(columns[j][0], j)
                pivots = jnp.where(sub == j, pivot, pivots)
                inv = 1.0 / pivot
                factors = [jnp.where(sub > j, columns[j][0], 0.0)] + columns[j][1:]
                for k in range(j + 1, SUB):
                    scaled = row_of(columns[k][0], j) * inv
                    columns[k] = [c - m * scaled for c, m in zip(columns[k], factors)]
                rows = [row_of(t, j) * inv for t in tiles[q]]
                for g in range(q, groups):
                    tiles[g] = [t - factors[g - q] * r for t, r in zip(tiles[g], rows)]
            scales.append(lax.rsqrt(pivots))
        tiles = [[t * scales[g] for t in tiles[g]] for g in range(groups)]
        parts = []
        for h in range(2):
            part = jnp.concatenate([tiles[g][h] for g in range(groups)], axis=0)
            if h == home:
                unit = jnp.concatenate([tiles[g][2] for g in range(groups)], axis=0)
                at = lax.broadcasted_iota(jnp.int32, (ROWS, LANES), 1)
                part = jnp.where((at >= shift) & (at < shift + ROWS), unit, part)
            parts.append(part)
        strip = jnp.concatenate(parts, axis=1)
        inverse[b] = jnp.where(wide < high, strip, 0.0)
        if b < BLOCKS - 1:
            h0, m0, l0 = split3(strip)
            right = jnp.concatenate([h0, m0, h0, m0, l0, h0], axis=0)
            left = jnp.concatenate([h0, h0, m0, m0, h0, l0], axis=0)[:, high:]

            def updated(rest, first, last):
                update = lax.dot_general(
                    left[:, first - high : last - high], right, TN, preferred_element_type=F32
                )
                at = lax.broadcasted_iota(jnp.int32, rest.shape, 1)
                return jnp.where((at >= low) & (at < high), 0.0, rest) - update

            strip = updated(gram[high : high + ROWS, :], high, high + ROWS)
            if b < BLOCKS - 2:
                gram[high + ROWS :, :] = updated(gram[high + ROWS :, :], high + ROWS, ALL)


def kernel(
    orbitals, connectivity, lower, upper, matrices_hbm, out,
    places, gather_at, scatter_at, face_to, matrices, field_a, field_b, border_a, border_b,
    part, rounded, rounded_border, pieces, terms,
    first_out, first_in, shared_out, shared_in,
    blocks, halves, half_in, along_x, along_y, rows_all, gram, inverse,
    load_sem, first_ssem, first_rsem, shared_ssem, shared_rsem, ring_ssem, ring_rsem,
    core_ssem, core_rsem, x_ssem, x_rsem, y_ssem, y_rsem, z_ssem, z_rsem, pair_ssem, pair_rsem,
):
    s, o = lax.axis_index("slab"), lax.axis_index("orb")
    core, y, x = lax.rem(s, 2), lax.rem(s // 2, SIDE), s // (2 * SIDE)
    other_core = s + 1 - 2 * core

    def slab_of(x_at, y_at, core_at):
        return (x_at * SIDE + y_at) * 2 + core_at

    def copy(source, target, ssem, rsem, **device):
        return pltpu.make_async_remote_copy(
            src_ref=source, dst_ref=target, send_sem=ssem, recv_sem=rsem,
            device_id=device, device_id_type=MESH,
        )

    up, down = lax.rem(s + 1, SLABS), lax.rem(s + SLABS - 1, SLABS)
    has = (s > 0, s < SLABS - 1)
    neighbour = (down, up)

    first_in[...] = jnp.zeros_like(first_in)
    shared_in[...] = jnp.zeros_like(shared_in)

    barrier = pltpu.get_barrier_semaphore()
    for d in range(1, BLOCKS):
        pl.semaphore_signal(
            barrier, inc=1, device_id={"orb": lax.rem(o + d, BLOCKS)}, device_id_type=MESH
        )
    for d in range(1, SIDE):
        for there in (
            slab_of(lax.rem(x + d, SIDE), y, core),
            slab_of(x, lax.rem(y + d, SIDE), core),
        ):
            pl.semaphore_signal(barrier, inc=1, device_id={"slab": there}, device_id_type=MESH)
    for there in neighbour:
        pl.semaphore_signal(barrier, inc=1, device_id={"slab": there}, device_id_type=MESH)

    load = pltpu.make_async_copy(matrices_hbm, matrices, load_sem)
    load.start()

    groups = [slice(g * PACK, (g + 1) * PACK) for g in range(ROWS // PACK)]
    local_tiles, side_tiles = LOCAL // LANES, FACE // LANES

    def span(t, width=LANES):
        return slice(t * width, (t + 1) * width)

    faces = jnp.concatenate([lower[...], upper[...]], axis=1)
    for j in range(2 * side_tiles):
        lane_at = jnp.broadcast_to(lane_of(faces[:, span(j)]), (SUB, LANES))
        tile_at = jnp.broadcast_to(tile_of(faces[:, span(j)]), (SUB, LANES))
        for g in range(ROWS // SUB):
            rows = span(g, SUB)
            values = pick_among(
                [(t, orbitals[rows, span(t)]) for t in range(OWN_TILES)],
                lane_at, tile_at, jnp.zeros((SUB, LANES), F32),
            )
            border_a[rows, span(j)] = values
            first_out[j // side_tiles, rows, span(j % side_tiles)] = values
    field_a[...] = orbitals[...]
    rounded[...] = orbitals[...].astype(BF16)

    found = find(faces)
    inverse_tables(found, OWN_TILES, face_to)
    for j in range(local_tiles):
        wanted = connectivity[:, span(j)]
        own = wanted - FACE
        face = jnp.full((CELLS, LANES), -1, jnp.int32)
        for t in range(OWN_TILES):
            row = found[t : t + 1] + LANES * (found[ROWS + t : ROWS + t + 1] - 1)
            face = pick_among(
                [(t, jnp.broadcast_to(row, (CELLS, LANES)))], lane_of(own), tile_of(own), face
            )
        place = jnp.where(face >= 0, face + OWN, own)
        place = jnp.where(wanted < FACE, wanted + (OWN + 2 * FACE), place)
        places[:, span(j)] = jnp.where(wanted >= OWN + FACE, wanted + 2 * FACE, place)

    def tables(c, _):
        wanted = places[pl.ds(c, 1), :]
        split_tables(wanted, gather_at.at[c])
        inverse_tables(find(wanted), TILES, scatter_at.at[c])
        return 0

    lax.fori_loop(0, CELLS, tables, 0)

    pl.semaphore_wait(barrier, BLOCKS - 1 + 2 * (SIDE - 1) + 2)

    def exchange(sent, received, ssem, rsem, *at):
        return [
            copy(
                sent.at[(*at, side)], received.at[(*at, 1 - side)],
                ssem.at[(*at, side)], rsem.at[(*at, 1 - side)], slab=neighbour[side],
            )
            for side in range(2)
        ]

    def start_both(copies):
        for side in range(2):
            pl.when(has[side])(copies[side].start)

    def land_both(copies):
        for side in range(2):
            pl.when(has[side])(copies[1 - side].wait_recv)

    def leave_both(copies):
        for side in range(2):
            pl.when(has[side])(copies[side].wait_send)

    first = exchange(first_out, first_in, first_ssem, first_rsem)
    start_both(first)

    nothing = jnp.zeros((PACK, LANES), BF16)

    def gather_own(i, _):
        for c in (2 * i, 2 * i + 1):
            for j in range(local_tiles):
                for rows in groups:
                    pieces[c, rows, span(j)] = pick_among(
                        [(t, rounded[rows, span(t)]) for t in range(OWN_TILES)],
                        gather_at[c, j, 0], gather_at[c, j, 1], nothing,
                    )
        return 0

    def multiply(i):
        for c in (2 * i, 2 * i + 1):
            parts = [
                jnp.concatenate(
                    [
                        pick_among(
                            [
                                (OWN_TILES + t, rounded_border[rows, span(t)])
                                for t in range(BORDER_TILES)
                            ],
                            gather_at[c, j, 0], gather_at[c, j, 1], pieces[c, rows, span(j)],
                        )
                        for rows in groups
                    ],
                    axis=0,
                )
                for j in range(local_tiles)
            ]
            terms[c] = jnp.dot(
                jnp.concatenate(parts, axis=1), matrices[c], preferred_element_type=F32
            ).astype(BF16)

    def gathered(t, g, cells):
        total = jnp.zeros((PACK, LANES), F32)
        for c in cells:
            total += pick_among(
                [(h, terms[c, groups[g], span(h)]) for h in range(local_tiles)],
                scatter_at[c, t, 0], scatter_at[c, t, 1], nothing,
            ).astype(F32)
        return total

    def add_border(i):
        for t in range(BORDER_TILES):
            for g, rows in enumerate(groups):
                part[rows, span(t)] += gathered(OWN_TILES + t, g, (2 * i, 2 * i + 1))

    def multiply_and_add(i, _):
        add_border(i - 1)
        multiply(i)
        return 0

    lax.fori_loop(0, CELLS // 2, gather_own, 0)
    load.wait()
    land_both(first)
    for side in range(2):
        border_a[:, span(2 + side, FACE)] = first_in[side]
    rounded_border[...] = border_a[...].astype(BF16)
    leave_both(first)

    fields, borders = [field_a, field_b], [border_a, border_b]
    for k in range(DEGREE):
        part[...] = jnp.zeros_like(part)
        multiply(0)
        lax.fori_loop(1, CELLS // 2, multiply_and_add, 0)
        add_border(CELLS // 2 - 1)
        for side in range(2):
            shared_out[k, side, 0] = part[:, span(2 + side, FACE)].astype(BF16)
            shared_out[k, side, 1] = part[:, span(side, FACE)].astype(BF16)
        copies = exchange(shared_out, shared_in, shared_ssem, shared_rsem, k)
        start_both(copies)

        target, target_border = fields[(k + 1) % 2], borders[(k + 1) % 2]

        def scatter_own(i, _):
            for t in range(STEP_TILES):
                t = STEP_TILES * i + t
                columns = pl.ds(pl.multiple_of(t * LANES, LANES), LANES)
                for g, rows in enumerate(groups):
                    total = gathered(t, g, range(CELLS))
                    if k > 0:
                        total = 2.0 * total - target[rows, columns]
                    target[rows, columns] = total
                    rounded[rows, columns] = total.astype(BF16)
            return 0

        lax.fori_loop(0, OWN_TILES // STEP_TILES, scatter_own, 0)
        if k < DEGREE - 1:
            lax.fori_loop(0, CELLS // 2, gather_own, 0)
        land_both(copies)
        for side in range(2):
            present = jnp.where(has[side], 1.0, 0.0)
            for kind, columns in enumerate((span(side, FACE), span(2 + side, FACE))):
                total = part[:, columns] + shared_in[k, side, kind].astype(F32)
                if kind == 1:
                    total = total * present
                if k > 0:
                    total = 2.0 * total - target_border[:, columns]
                target_border[:, columns] = total
                rounded_border[:, columns] = total.astype(BF16)
        leave_both(copies)

    for t in range(OWN_TILES):
        p, q = divmod(t, PIECE // LANES)
        for rows in groups:
            blocks[o, p, rows, span(q)] = pick_among(
                [(h, rounded_border[rows, span(h)]) for h in range(2 * side_tiles)],
                face_to[t, 0], face_to[t, 1], rounded[rows, span(t)],
            )

    def turn(at):
        return lax.rem(at + BLOCKS, BLOCKS)

    ways = (1, -1)
    far = BLOCKS // 2

    def moves(way, d, p):
        return d < far or (d == far and (p < PIECES // 2) == (way == 0))

    def ring(way, d, p):
        step = ways[way]
        held = blocks.at[turn(o - step * (d - 1)), p]
        return copy(
            held, held, ring_ssem.at[way, d - 1, p], ring_rsem.at[way, d - 1, p],
            orb=turn(o + step),
        )

    sent = []

    def relay(d):
        for p in range(PIECES):
            for way in range(2):
                if d > 1 and moves(way, d - 1, p):
                    ring(way, d - 1, p).wait_recv()
                if d <= far and moves(way, d, p):
                    one = ring(way, d, p)
                    one.start()
                    sent.append(one)

    for d in range(1, far):
        relay(d)

    quarter, share = lax.rem(o + 2, far), turn(o - 2) // far
    products = jnp.zeros((2 * ROWS + HALF, 5 * ROWS), F32)
    for p in range(PIECES):
        left = jnp.concatenate(
            [
                blocks[o, p], blocks[turn(o - 1), p],
                blocks[quarter, p, pl.ds(pl.multiple_of(share * HALF, HALF), HALF), :],
            ],
            axis=0,
        )
        right = jnp.concatenate(
            [blocks[turn(o + k), p] for k in (0, 1, 2, 1)] + [blocks[quarter + far, p]], axis=0
        )
        products += lax.dot_general(left, right, NT, preferred_element_type=F32)
    near = lax.broadcasted_iota(jnp.int32, (ROWS, LANES), 1) < 2 * ROWS
    strip = jnp.where(near, products[:ROWS, :LANES], products[ROWS : 2 * ROWS, :LANES])
    halves[0] = strip[:SHARED]
    halves[1, : ROWS - SHARED] = strip[SHARED:]
    halves[1, ROWS - SHARED :] = jnp.concatenate(
        [products[2 * ROWS :, LANES:], jnp.zeros((HALF, LANES - ROWS), F32)], axis=1
    )

    one = copy(halves.at[1 - core], half_in, core_ssem, core_rsem, slab=other_core)
    one.start()
    one.wait()
    along_x[0] = halves[core] + half_in[...]
    copies = [
        copy(
            along_x.at[0], along_x.at[d], x_ssem.at[d], x_rsem.at[d],
            slab=slab_of(lax.rem(x + d, SIDE), y, core),
        )
        for d in range(1, SIDE)
    ]
    for one in copies:
        one.start()
    for one in copies:
        one.wait()
    along_y[0] = (along_x[0] + along_x[1]) + (along_x[2] + along_x[3])
    relay(far)
    copies = [
        copy(
            along_y.at[0], along_y.at[d], y_ssem.at[d], y_rsem.at[d],
            slab=slab_of(x, lax.rem(y + d, SIDE), core),
        )
        for d in range(1, SIDE)
    ]
    for one in copies:
        one.start()
    for one in copies:
        one.wait()
    rows_all[core, o] = (along_y[0] + along_y[1]) + (along_y[2] + along_y[3])

    def pair(k):
        held = rows_all.at[core, k]
        return copy(held, held, pair_ssem.at[k], pair_rsem.at[k], slab=other_core)

    copies = [
        copy(
            rows_all.at[core, o], rows_all.at[core, o], z_ssem.at[d], z_rsem.at[d],
            orb=turn(o + d),
        )
        for d in range(1, BLOCKS)
    ]
    for d in (4, 3, 5, 2, 6, 1, 7):
        copies[d - 1].start()
    pair(o).start()
    for d in (1, 7, 2, 6, 3, 5, 4):
        copies[d - 1].wait_recv()
        pair(turn(o - d)).start()
    for k in range(BLOCKS):
        pair(k).wait()
    relay(far + 1)
    for one in copies + sent:
        one.wait_send()

    strips = [
        jnp.concatenate([rows_all[0, k], rows_all[1, k, : ROWS - SHARED]], axis=0)
        for k in range(BLOCKS)
    ]
    strips = [jnp.where(near, strips[k], strips[(k + 1) % BLOCKS]) for k in range(BLOCKS)]
    place = (0, 1, 3, 2)
    for i in range(BLOCKS):
        rows = span(i, ROWS)
        for j in range(i, BLOCKS):
            away = j - i
            if away < far:
                gram[rows, span(j, ROWS)] = strips[i][:, span(place[away], ROWS)]
            elif away > far:
                gram[rows, span(j, ROWS)] = strips[j][:, span(place[BLOCKS - away], ROWS)].T
            else:
                for half in range(2):
                    gram[i * ROWS + half * HALF : i * ROWS + (half + 1) * HALF, span(j, ROWS)] = (
                        rows_all[1, (i + 2 + half * far) % BLOCKS, ROWS - SHARED :, :ROWS]
                    )
    invert_factor(gram, inverse)

    weights = inverse[o] * math.sqrt(OWN * SLABS)
    upper = weights.astype(BF16)
    lower = (weights - upper.astype(F32)).astype(BF16)
    weights = jnp.concatenate([upper, lower], axis=0)
    for p in range(PIECES):
        both = jnp.dot(weights, blocks[:, p].reshape(ALL, PIECE), preferred_element_type=F32)
        out[:, p * PIECE : (p + 1) * PIECE] = both[:ROWS] + both[ROWS:]


def per_device(orbitals, cell_matrices, connectivity, face_lower, face_upper):
    vmem = pl.BlockSpec(memory_space=pltpu.VMEM)
    dma = pltpu.SemaphoreType.DMA
    return pl.pallas_call(
        kernel,
        out_shape=jax.ShapeDtypeStruct((ROWS, OWN), F32),
        in_specs=[vmem, vmem, vmem, vmem, pl.BlockSpec(memory_space=pl.ANY)],
        out_specs=vmem,
        scratch_shapes=[
            pltpu.VMEM((CELLS, LOCAL), jnp.int32),
            pltpu.VMEM((CELLS, LOCAL // LANES, 2, PACK, LANES), jnp.int16),
            pltpu.VMEM((CELLS, TILES, 2, PACK, LANES), jnp.int16),
            pltpu.VMEM((OWN_TILES, 2, PACK, LANES), jnp.int16),
            pltpu.VMEM((CELLS, LOCAL, LOCAL), BF16),
            pltpu.VMEM((ROWS, OWN), F32),
            pltpu.VMEM((ROWS, OWN), F32),
            pltpu.VMEM((ROWS, BORDER), F32),
            pltpu.VMEM((ROWS, BORDER), F32),
            pltpu.VMEM((ROWS, BORDER), F32),
            pltpu.VMEM((ROWS, OWN), BF16),
            pltpu.VMEM((ROWS, BORDER), BF16),
            pltpu.VMEM((CELLS, ROWS, LOCAL), BF16),
            pltpu.VMEM((CELLS, ROWS, LOCAL), BF16),
            pltpu.VMEM((2, ROWS, FACE), F32),
            pltpu.VMEM((2, ROWS, FACE), F32),
            pltpu.VMEM((DEGREE, 2, 2, ROWS, FACE), BF16),
            pltpu.VMEM((DEGREE, 2, 2, ROWS, FACE), BF16),
            pltpu.VMEM((BLOCKS, PIECES, ROWS, PIECE), BF16),
            pltpu.VMEM((2, SHARED, LANES), F32),
            pltpu.VMEM((SHARED, LANES), F32),
            pltpu.VMEM((SIDE, SHARED, LANES), F32),
            pltpu.VMEM((SIDE, SHARED, LANES), F32),
            pltpu.VMEM((2, BLOCKS, SHARED, LANES), F32),
            pltpu.VMEM((ALL, ALL), F32),
            pltpu.VMEM((BLOCKS, ROWS, ALL), F32),
            dma,
            dma((2,)), dma((2,)), dma((DEGREE, 2)), dma((DEGREE, 2)),
            dma((2, BLOCKS // 2, PIECES)), dma((2, BLOCKS // 2, PIECES)),
            dma, dma,
            dma((SIDE,)), dma((SIDE,)), dma((SIDE,)), dma((SIDE,)),
            dma((BLOCKS,)), dma((BLOCKS,)), dma((BLOCKS,)), dma((BLOCKS,)),
        ],
        compiler_params=pltpu.CompilerParams(collective_id=0, has_side_effects=True),
        name="filter_and_orthonormalize",
    )(orbitals, connectivity, face_lower[None, :], face_upper[None, :], cell_matrices)


def solution(mesh):
    in_specs = (P("orb", "slab"), P("slab", None, None), P("slab", None), P("slab"), P("slab"))
    return jax.shard_map(
        per_device, mesh=mesh, in_specs=in_specs, out_specs=P("orb", "slab"), check_vma=False
    )
```

```python
import functools
import math

import jax
import jax.numpy as jnp
from jax import lax
from jax.experimental import pallas as pl
from jax.experimental.pallas import tpu as pltpu
from jax.sharding import PartitionSpec as P

MESH = pl.DeviceIdType.MESH
F32, BF16 = jnp.float32, jnp.bfloat16
NT = (((1,), (1,)), ((), ()))
TN = (((0,), (0,)), ((), ()))

DEGREE = 4
CELLS = 8
LOCAL = 512
ROWS = 32
PACK = 16
SUB = 8
LANES = 128
OWN = 2048
FACE = 256
OWN_TILES = OWN // LANES
BORDER_TILES = 8
BORDER = BORDER_TILES * LANES
TILES = OWN_TILES + BORDER_TILES
BLOCKS = 8
SLABS = 32
SIDE = 4
STEP_TILES = 4
PIECES = 4
PIECE = OWN // PIECES
HALF = ROWS // 2
SHARED = (ROWS + HALF) // 2
ALL = ROWS * BLOCKS


def pick(tile, index):
    numbers = lax.GatherDimensionNumbers(
        offset_dims=(), collapsed_slice_dims=(1,), start_index_map=(1,),
        operand_batching_dims=(0,), start_indices_batching_dims=(0,),
    )
    return lax.gather(
        tile, index[..., None], numbers, (1, 1), mode=lax.GatherScatterMode.PROMISE_IN_BOUNDS
    )


def pick_among(tiles, lane_at, tile_at, start):
    for number, tile in tiles:
        start = jnp.where(tile_at == number, pick(tile, lane_at), start)
    return start


def spread(row):
    return jnp.broadcast_to(row, (PACK, LANES)).astype(jnp.int16)


def lane_of(position):
    return jnp.bitwise_and(position, LANES - 1)


def tile_of(position):
    return lax.shift_right_arithmetic(position, 7)


def split_tables(wanted, table):
    for j in range(LOCAL // LANES):
        part = wanted[:, j * LANES : (j + 1) * LANES]
        table[j, 0] = spread(lane_of(part))
        table[j, 1] = spread(tile_of(part))


def find(wanted):
    number = lax.broadcasted_iota(jnp.int32, (1, LOCAL), 1)
    at_tile = lax.broadcasted_iota(jnp.int32, (ROWS, LOCAL), 0) == tile_of(wanted)
    lanes = jnp.where(at_tile, lane_of(number).astype(F32), 0.0)
    numbers = jnp.where(at_tile, (tile_of(number) + 1).astype(F32), 0.0)
    at_lane = lax.broadcasted_iota(jnp.int32, (LANES, LOCAL), 0) == lane_of(wanted)
    return lax.dot_general(
        jnp.concatenate([lanes, numbers], axis=0).astype(BF16),
        jnp.where(at_lane, 1.0, 0.0).astype(BF16),
        NT, preferred_element_type=F32,
    ).astype(jnp.int32)


def inverse_tables(found, tiles, table):
    for t in range(tiles):
        table[t, 0] = spread(found[t : t + 1])
        table[t, 1] = spread(found[ROWS + t : ROWS + t + 1] - 1)


def split3(x):
    high = x.astype(BF16)
    rest = x - high.astype(F32)
    middle = rest.astype(BF16)
    low = (rest - middle.astype(F32)).astype(BF16)
    return high, middle, low


def invert_factor(gram, inverse):
    groups = ROWS // SUB
    sub = lax.broadcasted_iota(jnp.int32, (SUB, LANES), 0)
    lane = lax.broadcasted_iota(jnp.int32, (SUB, LANES), 1)
    wide = lax.broadcasted_iota(jnp.int32, (ROWS, ALL), 1)
    zero = jnp.zeros((SUB, LANES), F32)

    def row_of(tile, j):
        return jnp.broadcast_to(tile[j : j + 1, :], (SUB, LANES))

    def column_of(tile, j):
        return jnp.broadcast_to(tile[:, j : j + 1], (SUB, LANES))

    strip = gram[:ROWS, :]
    for b in range(BLOCKS):
        low, high = b * ROWS, (b + 1) * ROWS
        home, shift = low // LANES, low % LANES
        tiles = [
            [strip[g * SUB : (g + 1) * SUB, h * LANES : (h + 1) * LANES] for h in range(2)]
            + [jnp.where(lane - shift == sub + g * SUB, 1.0, 0.0)]
            for g in range(groups)
        ]
        scales = []
        for q in range(groups):
            columns = [
                [column_of(tiles[g][home], shift + q * SUB + k) for g in range(q, groups)]
                for k in range(SUB)
            ]
            pivots = zero
            for j in range(SUB):
                pivot = row_of(columns[j][0], j)
                pivots = jnp.where(sub == j, pivot, pivots)
                inv = 1.0 / pivot
                factors = [jnp.where(sub > j, columns[j][0], 0.0)] + columns[j][1:]
                for k in range(j + 1, SUB):
                    scaled = row_of(columns[k][0], j) * inv
                    columns[k] = [c - m * scaled for c, m in zip(columns[k], factors)]
                rows = [row_of(t, j) * inv for t in tiles[q]]
                for g in range(q, groups):
                    tiles[g] = [t - factors[g - q] * r for t, r in zip(tiles[g], rows)]
            scales.append(lax.rsqrt(pivots))
        tiles = [[t * scales[g] for t in tiles[g]] for g in range(groups)]
        parts = []
        for h in range(2):
            part = jnp.concatenate([tiles[g][h] for g in range(groups)], axis=0)
            if h == home:
                unit = jnp.concatenate([tiles[g][2] for g in range(groups)], axis=0)
                at = lax.broadcasted_iota(jnp.int32, (ROWS, LANES), 1)
                part = jnp.where((at >= shift) & (at < shift + ROWS), unit, part)
            parts.append(part)
        strip = jnp.concatenate(parts, axis=1)
        inverse[b] = jnp.where(wide < high, strip, 0.0)
        if b < BLOCKS - 1:
            h0, m0, l0 = split3(strip)
            right = jnp.concatenate([h0, m0, h0, m0, l0, h0], axis=0)
            left = jnp.concatenate([h0, h0, m0, m0, h0, l0], axis=0)[:, high:]

            def updated(rest, first, last):
                update = lax.dot_general(
                    left[:, first - high : last - high], right, TN, preferred_element_type=F32
                )
                at = lax.broadcasted_iota(jnp.int32, rest.shape, 1)
                return jnp.where((at >= low) & (at < high), 0.0, rest) - update

            strip = updated(gram[high : high + ROWS, :], high, high + ROWS)
            if b < BLOCKS - 2:
                gram[high + ROWS :, :] = updated(gram[high + ROWS :, :], high + ROWS, ALL)


def kernel(
    orbitals_hbm, connectivity_hbm, lower_hbm, upper_hbm, matrices_hbm, out,
    orbitals, connectivity, lower, upper,
    places, gather_at, scatter_at, face_to, matrices, field_a, field_b, border_a, border_b,
    part, rounded, rounded_border, pieces, terms,
    first_out, first_in, shared_out, shared_in,
    blocks, halves, half_in, along_x, along_y, rows_all, gram, inverse,
    load_sem, first_ssem, first_rsem, shared_ssem, shared_rsem, ring_ssem, ring_rsem,
    core_ssem, core_rsem, x_ssem, x_rsem, y_ssem, y_rsem, z_ssem, z_rsem, pair_ssem, pair_rsem,
):
    s, o = lax.axis_index("slab"), lax.axis_index("orb")
    core, y, x = lax.rem(s, 2), lax.rem(s // 2, SIDE), s // (2 * SIDE)
    other_core = s + 1 - 2 * core

    def slab_of(x_at, y_at, core_at):
        return (x_at * SIDE + y_at) * 2 + core_at

    def copy(source, target, ssem, rsem, **device):
        return pltpu.make_async_remote_copy(
            src_ref=source, dst_ref=target, send_sem=ssem, recv_sem=rsem,
            device_id=device, device_id_type=MESH,
        )

    up, down = lax.rem(s + 1, SLABS), lax.rem(s + SLABS - 1, SLABS)
    has = (s > 0, s < SLABS - 1)
    neighbour = (down, up)

    inputs = [
        pltpu.make_async_copy(source, held, load_sem.at[n])
        for n, (source, held) in enumerate(
            [
                (lower_hbm, lower), (upper_hbm, upper),
                (orbitals_hbm, orbitals), (connectivity_hbm, connectivity),
            ]
        )
    ]
    for one in inputs:
        one.start()
    first_in[...] = jnp.zeros_like(first_in)
    shared_in[...] = jnp.zeros_like(shared_in)

    barrier = pltpu.get_barrier_semaphore()
    for d in range(1, BLOCKS):
        pl.semaphore_signal(
            barrier, inc=1, device_id={"orb": lax.rem(o + d, BLOCKS)}, device_id_type=MESH
        )
    for d in range(1, SIDE):
        for there in (
            slab_of(lax.rem(x + d, SIDE), y, core),
            slab_of(x, lax.rem(y + d, SIDE), core),
        ):
            pl.semaphore_signal(barrier, inc=1, device_id={"slab": there}, device_id_type=MESH)
    for there in neighbour:
        pl.semaphore_signal(barrier, inc=1, device_id={"slab": there}, device_id_type=MESH)

    for one in inputs:
        one.wait()
    load = pltpu.make_async_copy(matrices_hbm, matrices, load_sem.at[4])
    load.start()

    groups = [slice(g * PACK, (g + 1) * PACK) for g in range(ROWS // PACK)]
    local_tiles, side_tiles = LOCAL // LANES, FACE // LANES

    def span(t, width=LANES):
        return slice(t * width, (t + 1) * width)

    faces = jnp.concatenate([lower[...], upper[...]], axis=1)
    for j in range(2 * side_tiles):
        lane_at = jnp.broadcast_to(lane_of(faces[:, span(j)]), (SUB, LANES))
        tile_at = jnp.broadcast_to(tile_of(faces[:, span(j)]), (SUB, LANES))
        for g in range(ROWS // SUB):
            rows = span(g, SUB)
            values = pick_among(
                [(t, orbitals[rows, span(t)]) for t in range(OWN_TILES)],
                lane_at, tile_at, jnp.zeros((SUB, LANES), F32),
            )
            border_a[rows, span(j)] = values
            first_out[j // side_tiles, rows, span(j % side_tiles)] = values
    field_a[...] = orbitals[...]
    rounded[...] = orbitals[...].astype(BF16)

    found = find(faces)
    inverse_tables(found, OWN_TILES, face_to)
    for j in range(local_tiles):
        wanted = connectivity[:, span(j)]
        own = wanted - FACE
        face = jnp.full((CELLS, LANES), -1, jnp.int32)
        for t in range(OWN_TILES):
            row = found[t : t + 1] + LANES * (found[ROWS + t : ROWS + t + 1] - 1)
            face = pick_among(
                [(t, jnp.broadcast_to(row, (CELLS, LANES)))], lane_of(own), tile_of(own), face
            )
        place = jnp.where(face >= 0, face + OWN, own)
        place = jnp.where(wanted < FACE, wanted + (OWN + 2 * FACE), place)
        places[:, span(j)] = jnp.where(wanted >= OWN + FACE, wanted + 2 * FACE, place)

    def tables(c, _):
        wanted = places[pl.ds(c, 1), :]
        split_tables(wanted, gather_at.at[c])
        inverse_tables(find(wanted), TILES, scatter_at.at[c])
        return 0

    lax.fori_loop(0, CELLS, tables, 0)

    pl.semaphore_wait(barrier, BLOCKS - 1 + 2 * (SIDE - 1) + 2)

    def exchange(sent, received, ssem, rsem, *at):
        return [
            copy(
                sent.at[(*at, side)], received.at[(*at, 1 - side)],
                ssem.at[(*at, side)], rsem.at[(*at, 1 - side)], slab=neighbour[side],
            )
            for side in range(2)
        ]

    def start_both(copies):
        for side in range(2):
            pl.when(has[side])(copies[side].start)

    def land_both(copies):
        for side in range(2):
            pl.when(has[side])(copies[1 - side].wait_recv)

    def leave_both(copies):
        for side in range(2):
            pl.when(has[side])(copies[side].wait_send)

    first = exchange(first_out, first_in, first_ssem, first_rsem)
    start_both(first)

    nothing = jnp.zeros((PACK, LANES), BF16)

    def gather_own(i, _):
        for c in (2 * i, 2 * i + 1):
            for j in range(local_tiles):
                for rows in groups:
                    pieces[c, rows, span(j)] = pick_among(
                        [(t, rounded[rows, span(t)]) for t in range(OWN_TILES)],
                        gather_at[c, j, 0], gather_at[c, j, 1], nothing,
                    )
        return 0

    def complete(i):
        for c in (2 * i, 2 * i + 1):
            for j in range(local_tiles):
                for rows in groups:
                    pieces[c, rows, span(j)] = pick_among(
                        [
                            (OWN_TILES + t, rounded_border[rows, span(t)])
                            for t in range(BORDER_TILES)
                        ],
                        gather_at[c, j, 0], gather_at[c, j, 1], pieces[c, rows, span(j)],
                    )

    def products_of(i):
        return [
            jnp.dot(pieces[c], matrices[c], preferred_element_type=F32).astype(BF16)
            for c in (2 * i, 2 * i + 1)
        ]

    def keep(i, products):
        for c, product in enumerate(products):
            terms[2 * i + c] = product

    def gathered(t, g, cells):
        total = jnp.zeros((PACK, LANES), F32)
        for c in cells:
            total += pick_among(
                [(h, terms[c, groups[g], span(h)]) for h in range(local_tiles)],
                scatter_at[c, t, 0], scatter_at[c, t, 1], nothing,
            ).astype(F32)
        return total

    def add_border(i):
        for t in range(BORDER_TILES):
            for g, rows in enumerate(groups):
                part[rows, span(t)] += gathered(OWN_TILES + t, g, (2 * i, 2 * i + 1))

    def middle(i, _):
        products = products_of(i)
        add_border(i - 1)
        complete(i + 1)
        keep(i, products)
        return 0

    lax.fori_loop(0, CELLS // 2, gather_own, 0)
    load.wait()
    land_both(first)
    for side in range(2):
        border_a[:, span(2 + side, FACE)] = first_in[side]
    rounded_border[...] = border_a[...].astype(BF16)
    leave_both(first)

    fields, borders = [field_a, field_b], [border_a, border_b]
    for k in range(DEGREE):
        part[...] = jnp.zeros_like(part)
        complete(0)
        products = products_of(0)
        complete(1)
        keep(0, products)
        lax.fori_loop(1, CELLS // 2 - 1, middle, 0)
        products = products_of(CELLS // 2 - 1)
        add_border(CELLS // 2 - 2)
        keep(CELLS // 2 - 1, products)
        add_border(CELLS // 2 - 1)
        for side in range(2):
            shared_out[k, side, 0] = part[:, span(2 + side, FACE)].astype(BF16)
            shared_out[k, side, 1] = part[:, span(side, FACE)].astype(BF16)
        copies = exchange(shared_out, shared_in, shared_ssem, shared_rsem, k)
        start_both(copies)

        target, target_border = fields[(k + 1) % 2], borders[(k + 1) % 2]

        def scatter_own(i, _):
            for t in range(STEP_TILES):
                t = STEP_TILES * i + t
                columns = pl.ds(pl.multiple_of(t * LANES, LANES), LANES)
                for g, rows in enumerate(groups):
                    total = gathered(t, g, range(CELLS))
                    if k > 0:
                        total = 2.0 * total - target[rows, columns]
                    target[rows, columns] = total
                    rounded[rows, columns] = total.astype(BF16)
            return 0

        lax.fori_loop(0, OWN_TILES // STEP_TILES, scatter_own, 0)
        if k < DEGREE - 1:
            lax.fori_loop(0, CELLS // 2, gather_own, 0)
        land_both(copies)
        for side in range(2):
            present = jnp.where(has[side], 1.0, 0.0)
            for kind, columns in enumerate((span(side, FACE), span(2 + side, FACE))):
                total = part[:, columns] + shared_in[k, side, kind].astype(F32)
                if kind == 1:
                    total = total * present
                if k > 0:
                    total = 2.0 * total - target_border[:, columns]
                target_border[:, columns] = total
                rounded_border[:, columns] = total.astype(BF16)
        leave_both(copies)

    for t in range(OWN_TILES):
        p, q = divmod(t, PIECE // LANES)
        for rows in groups:
            blocks[o, p, rows, span(q)] = pick_among(
                [(h, rounded_border[rows, span(h)]) for h in range(2 * side_tiles)],
                face_to[t, 0], face_to[t, 1], rounded[rows, span(t)],
            )

    def turn(at):
        return lax.rem(at + BLOCKS, BLOCKS)

    ways = (1, -1)
    far = BLOCKS // 2

    def moves(way, d, p):
        return d < far or (d == far and (p < PIECES // 2) == (way == 0))

    def ring(way, d, p):
        step = ways[way]
        held = blocks.at[turn(o - step * (d - 1)), p]
        return copy(
            held, held, ring_ssem.at[way, d - 1, p], ring_rsem.at[way, d - 1, p],
            orb=turn(o + step),
        )

    sent = []

    def relay(d, arrived=lambda p: None):
        for p in range(PIECES):
            for way in range(2):
                if d > 1 and moves(way, d - 1, p):
                    ring(way, d - 1, p).wait_recv()
                if d <= far and moves(way, d, p):
                    one = ring(way, d, p)
                    one.start()
                    sent.append(one)
            arrived(p)

    quarter, share = lax.rem(o + 2, far), turn(o - 2) // far
    sums = []

    def multiply_blocks(p):
        left = jnp.concatenate(
            [
                blocks[o, p], blocks[turn(o - 1), p],
                blocks[quarter, p, pl.ds(pl.multiple_of(share * HALF, HALF), HALF), :],
            ],
            axis=0,
        )
        right = jnp.concatenate(
            [blocks[turn(o + k), p] for k in (0, 1, 2, 1)] + [blocks[quarter + far, p]], axis=0
        )
        sums.append(lax.dot_general(left, right, NT, preferred_element_type=F32))

    relay(1)
    relay(2)
    relay(3, multiply_blocks)
    products = (sums[0] + sums[1]) + (sums[2] + sums[3])
    near = lax.broadcasted_iota(jnp.int32, (ROWS, LANES), 1) < 2 * ROWS
    strip = jnp.where(near, products[:ROWS, :LANES], products[ROWS : 2 * ROWS, :LANES])
    halves[0] = strip[:SHARED]
    halves[1, : ROWS - SHARED] = strip[SHARED:]
    halves[1, ROWS - SHARED :] = jnp.concatenate(
        [products[2 * ROWS :, LANES:], jnp.zeros((HALF, LANES - ROWS), F32)], axis=1
    )

    one = copy(halves.at[1 - core], half_in, core_ssem, core_rsem, slab=other_core)
    one.start()
    one.wait()
    along_x[0] = halves[core] + half_in[...]
    copies = [
        copy(
            along_x.at[0], along_x.at[d], x_ssem.at[d], x_rsem.at[d],
            slab=slab_of(lax.rem(x + d, SIDE), y, core),
        )
        for d in range(1, SIDE)
    ]
    for one in copies:
        one.start()
    for one in copies:
        one.wait()
    along_y[0] = (along_x[0] + along_x[1]) + (along_x[2] + along_x[3])
    relay(far)
    copies = [
        copy(
            along_y.at[0], along_y.at[d], y_ssem.at[d], y_rsem.at[d],
            slab=slab_of(x, lax.rem(y + d, SIDE), core),
        )
        for d in range(1, SIDE)
    ]
    for one in copies:
        one.start()
    for one in copies:
        one.wait()
    rows_all[core, o] = (along_y[0] + along_y[1]) + (along_y[2] + along_y[3])

    def pair(k):
        held = rows_all.at[core, k]
        return copy(held, held, pair_ssem.at[k], pair_rsem.at[k], slab=other_core)

    copies = [
        copy(
            rows_all.at[core, o], rows_all.at[core, o], z_ssem.at[d], z_rsem.at[d],
            orb=turn(o + d),
        )
        for d in range(1, BLOCKS)
    ]
    for d in (4, 3, 5, 2, 6, 1, 7):
        copies[d - 1].start()
    pair(o).start()
    for d in (1, 7, 2, 6, 3, 5, 4):
        copies[d - 1].wait_recv()
        pair(turn(o - d)).start()
    for k in range(BLOCKS):
        pair(k).wait()
    relay(far + 1)
    for one in copies + sent:
        one.wait_send()

    strips = [
        jnp.concatenate([rows_all[0, k], rows_all[1, k, : ROWS - SHARED]], axis=0)
        for k in range(BLOCKS)
    ]
    strips = [jnp.where(near, strips[k], strips[(k + 1) % BLOCKS]) for k in range(BLOCKS)]
    place = (0, 1, 3, 2)
    for i in range(BLOCKS):
        rows = span(i, ROWS)
        for j in range(i, BLOCKS):
            away = j - i
            if away < far:
                gram[rows, span(j, ROWS)] = strips[i][:, span(place[away], ROWS)]
            elif away > far:
                gram[rows, span(j, ROWS)] = strips[j][:, span(place[BLOCKS - away], ROWS)].T
            else:
                for half in range(2):
                    gram[i * ROWS + half * HALF : i * ROWS + (half + 1) * HALF, span(j, ROWS)] = (
                        rows_all[1, (i + 2 + half * far) % BLOCKS, ROWS - SHARED :, :ROWS]
                    )
    invert_factor(gram, inverse)

    weights = inverse[o] * math.sqrt(OWN * SLABS)
    upper = weights.astype(BF16)
    lower = (weights - upper.astype(F32)).astype(BF16)
    weights = jnp.concatenate([upper, lower], axis=0)
    for p in range(PIECES):
        both = jnp.dot(weights, blocks[:, p].reshape(ALL, PIECE), preferred_element_type=F32)
        out[:, p * PIECE : (p + 1) * PIECE] = both[:ROWS] + both[ROWS:]


def per_device(orbitals, cell_matrices, connectivity, face_lower, face_upper):
    vmem = pl.BlockSpec(memory_space=pltpu.VMEM)
    dma = pltpu.SemaphoreType.DMA
    return pl.pallas_call(
        kernel,
        out_shape=jax.ShapeDtypeStruct((ROWS, OWN), F32),
        in_specs=[pl.BlockSpec(memory_space=pl.ANY)] * 5,
        out_specs=vmem,
        scratch_shapes=[
            pltpu.VMEM((ROWS, OWN), F32),
            pltpu.VMEM((CELLS, LOCAL), jnp.int32),
            pltpu.VMEM((1, FACE), jnp.int32),
            pltpu.VMEM((1, FACE), jnp.int32),
            pltpu.VMEM((CELLS, LOCAL), jnp.int32),
            pltpu.VMEM((CELLS, LOCAL // LANES, 2, PACK, LANES), jnp.int16),
            pltpu.VMEM((CELLS, TILES, 2, PACK, LANES), jnp.int16),
            pltpu.VMEM((OWN_TILES, 2, PACK, LANES), jnp.int16),
            pltpu.VMEM((CELLS, LOCAL, LOCAL), BF16),
            pltpu.VMEM((ROWS, OWN), F32),
            pltpu.VMEM((ROWS, OWN), F32),
            pltpu.VMEM((ROWS, BORDER), F32),
            pltpu.VMEM((ROWS, BORDER), F32),
            pltpu.VMEM((ROWS, BORDER), F32),
            pltpu.VMEM((ROWS, OWN), BF16),
            pltpu.VMEM((ROWS, BORDER), BF16),
            pltpu.VMEM((CELLS, ROWS, LOCAL), BF16),
            pltpu.VMEM((CELLS, ROWS, LOCAL), BF16),
            pltpu.VMEM((2, ROWS, FACE), F32),
            pltpu.VMEM((2, ROWS, FACE), F32),
            pltpu.VMEM((DEGREE, 2, 2, ROWS, FACE), BF16),
            pltpu.VMEM((DEGREE, 2, 2, ROWS, FACE), BF16),
            pltpu.VMEM((BLOCKS, PIECES, ROWS, PIECE), BF16),
            pltpu.VMEM((2, SHARED, LANES), F32),
            pltpu.VMEM((SHARED, LANES), F32),
            pltpu.VMEM((SIDE, SHARED, LANES), F32),
            pltpu.VMEM((SIDE, SHARED, LANES), F32),
            pltpu.VMEM((2, BLOCKS, SHARED, LANES), F32),
            pltpu.VMEM((ALL, ALL), F32),
            pltpu.VMEM((BLOCKS, ROWS, ALL), F32),
            dma((5,)),
            dma((2,)), dma((2,)), dma((DEGREE, 2)), dma((DEGREE, 2)),
            dma((2, BLOCKS // 2, PIECES)), dma((2, BLOCKS // 2, PIECES)),
            dma, dma,
            dma((SIDE,)), dma((SIDE,)), dma((SIDE,)), dma((SIDE,)),
            dma((BLOCKS,)), dma((BLOCKS,)), dma((BLOCKS,)), dma((BLOCKS,)),
        ],
        compiler_params=pltpu.CompilerParams(collective_id=0, has_side_effects=True),
        name="filter_and_orthonormalize",
    )(orbitals, connectivity, face_lower[None, :], face_upper[None, :], cell_matrices)


def solution(mesh):
    in_specs = (P("orb", "slab"), P("slab", None, None), P("slab", None), P("slab"), P("slab"))
    return jax.shard_map(
        per_device, mesh=mesh, in_specs=in_specs, out_specs=P("orb", "slab"), check_vma=False
    )
```

```python
import functools
import math

import jax
import jax.numpy as jnp
from jax import lax
from jax.experimental import pallas as pl
from jax.experimental.pallas import tpu as pltpu
from jax.sharding import PartitionSpec as P

MESH = pl.DeviceIdType.MESH
F32, BF16 = jnp.float32, jnp.bfloat16
NT = (((1,), (1,)), ((), ()))
TN = (((0,), (0,)), ((), ()))

DEGREE = 4
CELLS = 8
LOCAL = 512
ROWS = 32
PACK = 16
SUB = 8
LANES = 128
OWN = 2048
FACE = 256
OWN_TILES = OWN // LANES
BORDER_TILES = 8
BORDER = BORDER_TILES * LANES
TILES = OWN_TILES + BORDER_TILES
BLOCKS = 8
SLABS = 32
SIDE = 4
DENSE = 4
SPARSE = OWN // LANES - DENSE
STEPS = 4
PIECES = 4
PIECE = OWN // PIECES
HALF = ROWS // 2
SHARED = (ROWS + HALF) // 2
ALL = ROWS * BLOCKS


def pick(tile, index):
    numbers = lax.GatherDimensionNumbers(
        offset_dims=(), collapsed_slice_dims=(1,), start_index_map=(1,),
        operand_batching_dims=(0,), start_indices_batching_dims=(0,),
    )
    return lax.gather(
        tile, index[..., None], numbers, (1, 1), mode=lax.GatherScatterMode.PROMISE_IN_BOUNDS
    )


def pick_among(tiles, lane_at, tile_at, start):
    for number, tile in tiles:
        start = jnp.where(tile_at == number, pick(tile, lane_at), start)
    return start


def spread(row):
    return jnp.broadcast_to(row, (PACK, LANES)).astype(jnp.int16)


def lane_of(position):
    return jnp.bitwise_and(position, LANES - 1)


def tile_of(position):
    return lax.shift_right_arithmetic(position, 7)


def split_tables(wanted, table):
    for j in range(LOCAL // LANES):
        part = wanted[:, j * LANES : (j + 1) * LANES]
        table[j, 0] = spread(lane_of(part))
        table[j, 1] = spread(tile_of(part))


def find(wanted):
    number = lax.broadcasted_iota(jnp.int32, (1, LOCAL), 1)
    at_tile = lax.broadcasted_iota(jnp.int32, (ROWS, LOCAL), 0) == tile_of(wanted)
    lanes = jnp.where(at_tile, lane_of(number).astype(F32), 0.0)
    numbers = jnp.where(at_tile, (tile_of(number) + 1).astype(F32), 0.0)
    at_lane = lax.broadcasted_iota(jnp.int32, (LANES, LOCAL), 0) == lane_of(wanted)
    return lax.dot_general(
        jnp.concatenate([lanes, numbers], axis=0).astype(BF16),
        jnp.where(at_lane, 1.0, 0.0).astype(BF16),
        NT, preferred_element_type=F32,
    ).astype(jnp.int32)


def inverse_tables(found, tiles, table):
    for t in range(tiles):
        table[t, 0] = spread(found[t : t + 1])
        table[t, 1] = spread(found[ROWS + t : ROWS + t + 1] - 1)


def split3(x):
    high = x.astype(BF16)
    rest = x - high.astype(F32)
    middle = rest.astype(BF16)
    low = (rest - middle.astype(F32)).astype(BF16)
    return high, middle, low


def invert_factor(gram, inverse):
    groups = ROWS // SUB
    sub = lax.broadcasted_iota(jnp.int32, (SUB, LANES), 0)
    lane = lax.broadcasted_iota(jnp.int32, (SUB, LANES), 1)
    wide = lax.broadcasted_iota(jnp.int32, (ROWS, ALL), 1)
    zero = jnp.zeros((SUB, LANES), F32)

    def row_of(tile, j):
        return jnp.broadcast_to(tile[j : j + 1, :], (SUB, LANES))

    def column_of(tile, j):
        return jnp.broadcast_to(tile[:, j : j + 1], (SUB, LANES))

    strip = gram[:ROWS, :]
    for b in range(BLOCKS):
        low, high = b * ROWS, (b + 1) * ROWS
        home, shift = low // LANES, low % LANES
        tiles = [
            [strip[g * SUB : (g + 1) * SUB, h * LANES : (h + 1) * LANES] for h in range(2)]
            + [jnp.where(lane - shift == sub + g * SUB, 1.0, 0.0)]
            for g in range(groups)
        ]
        scales = []
        for q in range(groups):
            columns = [
                [column_of(tiles[g][home], shift + q * SUB + k) for g in range(q, groups)]
                for k in range(SUB)
            ]
            pivots = zero
            for j in range(SUB):
                pivot = row_of(columns[j][0], j)
                pivots = jnp.where(sub == j, pivot, pivots)
                inv = 1.0 / pivot
                factors = [jnp.where(sub > j, columns[j][0], 0.0)] + columns[j][1:]
                for k in range(j + 1, SUB):
                    scaled = row_of(columns[k][0], j) * inv
                    columns[k] = [c - m * scaled for c, m in zip(columns[k], factors)]
                rows = [row_of(t, j) * inv for t in tiles[q]]
                for g in range(q, groups):
                    tiles[g] = [t - factors[g - q] * r for t, r in zip(tiles[g], rows)]
            scales.append(lax.rsqrt(pivots))
        tiles = [[t * scales[g] for t in tiles[g]] for g in range(groups)]
        parts = []
        for h in range(2):
            part = jnp.concatenate([tiles[g][h] for g in range(groups)], axis=0)
            if h == home:
                unit = jnp.concatenate([tiles[g][2] for g in range(groups)], axis=0)
                at = lax.broadcasted_iota(jnp.int32, (ROWS, LANES), 1)
                part = jnp.where((at >= shift) & (at < shift + ROWS), unit, part)
            parts.append(part)
        strip = jnp.concatenate(parts, axis=1)
        inverse[b] = jnp.where(wide < high, strip, 0.0)
        if b < BLOCKS - 1:
            h0, m0, l0 = split3(strip)
            right = jnp.concatenate([h0, m0, h0, m0, l0, h0], axis=0)
            left = jnp.concatenate([h0, h0, m0, m0, h0, l0], axis=0)[:, high:]

            def updated(rest, first, last):
                update = lax.dot_general(
                    left[:, first - high : last - high], right, TN, preferred_element_type=F32
                )
                at = lax.broadcasted_iota(jnp.int32, rest.shape, 1)
                return jnp.where((at >= low) & (at < high), 0.0, rest) - update

            strip = updated(gram[high : high + ROWS, :], high, high + ROWS)
            if b < BLOCKS - 2:
                gram[high + ROWS :, :] = updated(gram[high + ROWS :, :], high + ROWS, ALL)


def kernel(
    orbitals_hbm, connectivity_hbm, lower_hbm, upper_hbm, matrices_hbm, out,
    orbitals, connectivity, lower, upper,
    places, gather_at, scatter_at, face_to, picker, dense, matrices, field_a, field_b, border_a, border_b,
    part, rounded, rounded_border, pieces, terms,
    first_out, first_in, shared_out, shared_in,
    blocks, halves, half_in, along_x, along_y, rows_all, gram, inverse,
    load_sem, first_ssem, first_rsem, shared_ssem, shared_rsem, ring_ssem, ring_rsem,
    core_ssem, core_rsem, x_ssem, x_rsem, y_ssem, y_rsem, z_ssem, z_rsem, pair_ssem, pair_rsem,
):
    s, o = lax.axis_index("slab"), lax.axis_index("orb")
    core, y, x = lax.rem(s, 2), lax.rem(s // 2, SIDE), s // (2 * SIDE)
    other_core = s + 1 - 2 * core

    def slab_of(x_at, y_at, core_at):
        return (x_at * SIDE + y_at) * 2 + core_at

    def copy(source, target, ssem, rsem, **device):
        return pltpu.make_async_remote_copy(
            src_ref=source, dst_ref=target, send_sem=ssem, recv_sem=rsem,
            device_id=device, device_id_type=MESH,
        )

    up, down = lax.rem(s + 1, SLABS), lax.rem(s + SLABS - 1, SLABS)
    has = (s > 0, s < SLABS - 1)
    neighbour = (down, up)

    inputs = [
        pltpu.make_async_copy(source, held, load_sem.at[n])
        for n, (source, held) in enumerate(
            [
                (lower_hbm, lower), (upper_hbm, upper),
                (orbitals_hbm, orbitals), (connectivity_hbm, connectivity),
            ]
        )
    ]
    for one in inputs:
        one.start()
    first_in[...] = jnp.zeros_like(first_in)
    shared_in[...] = jnp.zeros_like(shared_in)

    barrier = pltpu.get_barrier_semaphore()
    for d in range(1, BLOCKS):
        pl.semaphore_signal(
            barrier, inc=1, device_id={"orb": lax.rem(o + d, BLOCKS)}, device_id_type=MESH
        )
    for d in range(1, SIDE):
        for there in (
            slab_of(lax.rem(x + d, SIDE), y, core),
            slab_of(x, lax.rem(y + d, SIDE), core),
        ):
            pl.semaphore_signal(barrier, inc=1, device_id={"slab": there}, device_id_type=MESH)
    for there in neighbour:
        pl.semaphore_signal(barrier, inc=1, device_id={"slab": there}, device_id_type=MESH)

    for one in inputs:
        one.wait()
    load = pltpu.make_async_copy(matrices_hbm, matrices, load_sem.at[4])
    load.start()

    groups = [slice(g * PACK, (g + 1) * PACK) for g in range(ROWS // PACK)]
    local_tiles, side_tiles = LOCAL // LANES, FACE // LANES

    def span(t, width=LANES):
        return slice(t * width, (t + 1) * width)

    faces = jnp.concatenate([lower[...], upper[...]], axis=1)
    for j in range(2 * side_tiles):
        lane_at = jnp.broadcast_to(lane_of(faces[:, span(j)]), (SUB, LANES))
        tile_at = jnp.broadcast_to(tile_of(faces[:, span(j)]), (SUB, LANES))
        for g in range(ROWS // SUB):
            rows = span(g, SUB)
            values = pick_among(
                [(t, orbitals[rows, span(t)]) for t in range(OWN_TILES)],
                lane_at, tile_at, jnp.zeros((SUB, LANES), F32),
            )
            border_a[rows, span(j)] = values
            first_out[j // side_tiles, rows, span(j % side_tiles)] = values
    field_a[...] = orbitals[...]
    rounded[...] = orbitals[...].astype(BF16)

    found = find(faces)
    inverse_tables(found, OWN_TILES, face_to)
    for j in range(local_tiles):
        wanted = connectivity[:, span(j)]
        own = wanted - FACE
        face = jnp.full((CELLS, LANES), -1, jnp.int32)
        for t in range(OWN_TILES):
            row = found[t : t + 1] + LANES * (found[ROWS + t : ROWS + t + 1] - 1)
            face = pick_among(
                [(t, jnp.broadcast_to(row, (CELLS, LANES)))], lane_of(own), tile_of(own), face
            )
        place = jnp.where(face >= 0, face + OWN, own)
        place = jnp.where(wanted < FACE, wanted + (OWN + 2 * FACE), place)
        places[:, span(j)] = jnp.where(wanted >= OWN + FACE, wanted + 2 * FACE, place)

    def tables(c, _):
        wanted = places[pl.ds(c, 1), :]
        split_tables(wanted, gather_at.at[c])
        inverse_tables(find(wanted), TILES, scatter_at.at[c])
        return 0

    lax.fori_loop(0, CELLS, tables, 0)

    pl.semaphore_wait(barrier, BLOCKS - 1 + 2 * (SIDE - 1) + 2)

    def exchange(sent, received, ssem, rsem, *at):
        return [
            copy(
                sent.at[(*at, side)], received.at[(*at, 1 - side)],
                ssem.at[(*at, side)], rsem.at[(*at, 1 - side)], slab=neighbour[side],
            )
            for side in range(2)
        ]

    def start_both(copies):
        for side in range(2):
            pl.when(has[side])(copies[side].start)

    def land_both(copies):
        for side in range(2):
            pl.when(has[side])(copies[1 - side].wait_recv)

    def leave_both(copies):
        for side in range(2):
            pl.when(has[side])(copies[side].wait_send)

    first = exchange(first_out, first_in, first_ssem, first_rsem)
    start_both(first)

    def pick_dense(c, _):
        first_row = SPARSE * LANES
        wanted = places[pl.ds(c, 1), :] - first_row
        numbers = lax.broadcasted_iota(jnp.int32, (DENSE * LANES, LOCAL), 0)
        picker[c] = jnp.where(numbers == wanted, 1.0, 0.0).astype(BF16)
        return 0

    lax.fori_loop(0, CELLS, pick_dense, 0)

    nothing = jnp.zeros((PACK, LANES), BF16)

    def gather_own(i, _):
        for c in (2 * i, 2 * i + 1):
            exact = jnp.dot(
                rounded[:, SPARSE * LANES :], picker[c], preferred_element_type=F32
            ).astype(BF16)
            for j in range(local_tiles):
                for rows in groups:
                    pieces[c, rows, span(j)] = pick_among(
                        [(t, rounded[rows, span(t)]) for t in range(SPARSE)],
                        gather_at[c, j, 0], gather_at[c, j, 1], nothing,
                    ) + exact[rows, span(j)]
        return 0

    def complete(i):
        for c in (2 * i, 2 * i + 1):
            for j in range(local_tiles):
                for rows in groups:
                    pieces[c, rows, span(j)] = pick_among(
                        [
                            (OWN_TILES + t, rounded_border[rows, span(t)])
                            for t in range(BORDER_TILES)
                        ],
                        gather_at[c, j, 0], gather_at[c, j, 1], pieces[c, rows, span(j)],
                    )

    def products_of(i):
        return [
            jnp.dot(pieces[c], matrices[c], preferred_element_type=F32).astype(BF16)
            for c in (2 * i, 2 * i + 1)
        ]

    def keep(i, products):
        for c, product in enumerate(products):
            terms[2 * i + c] = product

    def gathered(t, g, cells):
        total = jnp.zeros((PACK, LANES), F32)
        for c in cells:
            total += pick_among(
                [(h, terms[c, groups[g], span(h)]) for h in range(local_tiles)],
                scatter_at[c, t, 0], scatter_at[c, t, 1], nothing,
            ).astype(F32)
        return total

    def add_border(i):
        for t in range(BORDER_TILES):
            for g, rows in enumerate(groups):
                part[rows, span(t)] += gathered(OWN_TILES + t, g, (2 * i, 2 * i + 1))

    def middle(i, _):
        products = products_of(i)
        add_border(i - 1)
        complete(i + 1)
        keep(i, products)
        return 0

    lax.fori_loop(0, CELLS // 2, gather_own, 0)
    load.wait()
    land_both(first)
    for side in range(2):
        border_a[:, span(2 + side, FACE)] = first_in[side]
    rounded_border[...] = border_a[...].astype(BF16)
    leave_both(first)

    fields, borders = [field_a, field_b], [border_a, border_b]
    for k in range(DEGREE):
        part[...] = jnp.zeros_like(part)
        complete(0)
        products = products_of(0)
        complete(1)
        keep(0, products)
        lax.fori_loop(1, CELLS // 2 - 1, middle, 0)
        products = products_of(CELLS // 2 - 1)
        add_border(CELLS // 2 - 2)
        keep(CELLS // 2 - 1, products)
        add_border(CELLS // 2 - 1)
        for side in range(2):
            shared_out[k, side, 0] = part[:, span(2 + side, FACE)].astype(BF16)
            shared_out[k, side, 1] = part[:, span(side, FACE)].astype(BF16)
        copies = exchange(shared_out, shared_in, shared_ssem, shared_rsem, k)
        start_both(copies)

        target, target_border = fields[(k + 1) % 2], borders[(k + 1) % 2]

        def advance(rows, columns, total):
            if k > 0:
                total = 2.0 * total - target[rows, columns]
            target[rows, columns] = total
            rounded[rows, columns] = total.astype(BF16)

        def scatter_own(i, total):
            for c in (2 * i, 2 * i + 1):
                total += lax.dot_general(terms[c], picker[c], NT, preferred_element_type=F32)
            for t in range(SPARSE // STEPS):
                t = SPARSE // STEPS * i + t
                columns = pl.ds(pl.multiple_of(t * LANES, LANES), LANES)
                for g, rows in enumerate(groups):
                    advance(rows, columns, gathered(t, g, range(CELLS)))
            return total

        dense[...] = lax.fori_loop(
            0, STEPS, scatter_own, jnp.zeros((ROWS, DENSE * LANES), F32)
        )
        advance(slice(None), slice(SPARSE * LANES, OWN), dense[...])
        if k < DEGREE - 1:
            lax.fori_loop(0, CELLS // 2, gather_own, 0)
        land_both(copies)
        for side in range(2):
            present = jnp.where(has[side], 1.0, 0.0)
            for kind, columns in enumerate((span(side, FACE), span(2 + side, FACE))):
                total = part[:, columns] + shared_in[k, side, kind].astype(F32)
                if kind == 1:
                    total = total * present
                if k > 0:
                    total = 2.0 * total - target_border[:, columns]
                target_border[:, columns] = total
                rounded_border[:, columns] = total.astype(BF16)
        leave_both(copies)

    for t in range(OWN_TILES):
        p, q = divmod(t, PIECE // LANES)
        for rows in groups:
            blocks[o, p, rows, span(q)] = pick_among(
                [(h, rounded_border[rows, span(h)]) for h in range(2 * side_tiles)],
                face_to[t, 0], face_to[t, 1], rounded[rows, span(t)],
            )

    def turn(at):
        return lax.rem(at + BLOCKS, BLOCKS)

    ways = (1, -1)
    far = BLOCKS // 2

    def moves(way, d, p):
        return d < far or (d == far and (p < PIECES // 2) == (way == 0))

    def ring(way, d, p):
        step = ways[way]
        held = blocks.at[turn(o - step * (d - 1)), p]
        return copy(
            held, held, ring_ssem.at[way, d - 1, p], ring_rsem.at[way, d - 1, p],
            orb=turn(o + step),
        )

    sent = []

    def relay(d, arrived=lambda p: None):
        for p in range(PIECES):
            for way in range(2):
                if d > 1 and moves(way, d - 1, p):
                    ring(way, d - 1, p).wait_recv()
                if d <= far and moves(way, d, p):
                    one = ring(way, d, p)
                    one.start()
                    sent.append(one)
            arrived(p)

    quarter, share = lax.rem(o + 2, far), turn(o - 2) // far
    sums = []

    def multiply_blocks(p):
        left = jnp.concatenate(
            [
                blocks[o, p], blocks[turn(o - 1), p],
                blocks[quarter, p, pl.ds(pl.multiple_of(share * HALF, HALF), HALF), :],
            ],
            axis=0,
        )
        right = jnp.concatenate(
            [blocks[turn(o + k), p] for k in (0, 1, 2, 1)] + [blocks[quarter + far, p]], axis=0
        )
        sums.append(lax.dot_general(left, right, NT, preferred_element_type=F32))

    relay(1)
    relay(2)
    relay(3, multiply_blocks)
    products = (sums[0] + sums[1]) + (sums[2] + sums[3])
    near = lax.broadcasted_iota(jnp.int32, (ROWS, LANES), 1) < 2 * ROWS
    strip = jnp.where(near, products[:ROWS, :LANES], products[ROWS : 2 * ROWS, :LANES])
    halves[0] = strip[:SHARED]
    halves[1, : ROWS - SHARED] = strip[SHARED:]
    halves[1, ROWS - SHARED :] = jnp.concatenate(
        [products[2 * ROWS :, LANES:], jnp.zeros((HALF, LANES - ROWS), F32)], axis=1
    )

    one = copy(halves.at[1 - core], half_in, core_ssem, core_rsem, slab=other_core)
    one.start()
    one.wait()
    along_x[0] = halves[core] + half_in[...]
    copies = [
        copy(
            along_x.at[0], along_x.at[d], x_ssem.at[d], x_rsem.at[d],
            slab=slab_of(lax.rem(x + d, SIDE), y, core),
        )
        for d in range(1, SIDE)
    ]
    for one in copies:
        one.start()
    for one in copies:
        one.wait()
    along_y[0] = (along_x[0] + along_x[1]) + (along_x[2] + along_x[3])
    relay(far)
    copies = [
        copy(
            along_y.at[0], along_y.at[d], y_ssem.at[d], y_rsem.at[d],
            slab=slab_of(x, lax.rem(y + d, SIDE), core),
        )
        for d in range(1, SIDE)
    ]
    for one in copies:
        one.start()
    for one in copies:
        one.wait()
    rows_all[core, o] = (along_y[0] + along_y[1]) + (along_y[2] + along_y[3])

    def pair(k):
        held = rows_all.at[core, k]
        return copy(held, held, pair_ssem.at[k], pair_rsem.at[k], slab=other_core)

    copies = [
        copy(
            rows_all.at[core, o], rows_all.at[core, o], z_ssem.at[d], z_rsem.at[d],
            orb=turn(o + d),
        )
        for d in range(1, BLOCKS)
    ]
    for d in (4, 3, 5, 2, 6, 1, 7):
        copies[d - 1].start()
    pair(o).start()
    for d in (1, 7, 2, 6, 3, 5, 4):
        copies[d - 1].wait_recv()
        pair(turn(o - d)).start()
    for k in range(BLOCKS):
        pair(k).wait()
    relay(far + 1)
    for one in copies + sent:
        one.wait_send()

    strips = [
        jnp.concatenate([rows_all[0, k], rows_all[1, k, : ROWS - SHARED]], axis=0)
        for k in range(BLOCKS)
    ]
    strips = [jnp.where(near, strips[k], strips[(k + 1) % BLOCKS]) for k in range(BLOCKS)]
    place = (0, 1, 3, 2)
    for i in range(BLOCKS):
        rows = span(i, ROWS)
        for j in range(i, BLOCKS):
            away = j - i
            if away < far:
                gram[rows, span(j, ROWS)] = strips[i][:, span(place[away], ROWS)]
            elif away > far:
                gram[rows, span(j, ROWS)] = strips[j][:, span(place[BLOCKS - away], ROWS)].T
            else:
                for half in range(2):
                    gram[i * ROWS + half * HALF : i * ROWS + (half + 1) * HALF, span(j, ROWS)] = (
                        rows_all[1, (i + 2 + half * far) % BLOCKS, ROWS - SHARED :, :ROWS]
                    )
    invert_factor(gram, inverse)

    weights = inverse[o] * math.sqrt(OWN * SLABS)
    upper = weights.astype(BF16)
    lower = (weights - upper.astype(F32)).astype(BF16)
    weights = jnp.concatenate([upper, lower], axis=0)
    for p in range(PIECES):
        both = jnp.dot(weights, blocks[:, p].reshape(ALL, PIECE), preferred_element_type=F32)
        out[:, p * PIECE : (p + 1) * PIECE] = both[:ROWS] + both[ROWS:]


def per_device(orbitals, cell_matrices, connectivity, face_lower, face_upper):
    vmem = pl.BlockSpec(memory_space=pltpu.VMEM)
    dma = pltpu.SemaphoreType.DMA
    return pl.pallas_call(
        kernel,
        out_shape=jax.ShapeDtypeStruct((ROWS, OWN), F32),
        in_specs=[pl.BlockSpec(memory_space=pl.ANY)] * 5,
        out_specs=vmem,
        scratch_shapes=[
            pltpu.VMEM((ROWS, OWN), F32),
            pltpu.VMEM((CELLS, LOCAL), jnp.int32),
            pltpu.VMEM((1, FACE), jnp.int32),
            pltpu.VMEM((1, FACE), jnp.int32),
            pltpu.VMEM((CELLS, LOCAL), jnp.int32),
            pltpu.VMEM((CELLS, LOCAL // LANES, 2, PACK, LANES), jnp.int16),
            pltpu.VMEM((CELLS, TILES, 2, PACK, LANES), jnp.int16),
            pltpu.VMEM((OWN_TILES, 2, PACK, LANES), jnp.int16),
            pltpu.VMEM((CELLS, DENSE * LANES, LOCAL), BF16),
            pltpu.VMEM((ROWS, DENSE * LANES), F32),
            pltpu.VMEM((CELLS, LOCAL, LOCAL), BF16),
            pltpu.VMEM((ROWS, OWN), F32),
            pltpu.VMEM((ROWS, OWN), F32),
            pltpu.VMEM((ROWS, BORDER), F32),
            pltpu.VMEM((ROWS, BORDER), F32),
            pltpu.VMEM((ROWS, BORDER), F32),
            pltpu.VMEM((ROWS, OWN), BF16),
            pltpu.VMEM((ROWS, BORDER), BF16),
            pltpu.VMEM((CELLS, ROWS, LOCAL), BF16),
            pltpu.VMEM((CELLS, ROWS, LOCAL), BF16),
            pltpu.VMEM((2, ROWS, FACE), F32),
            pltpu.VMEM((2, ROWS, FACE), F32),
            pltpu.VMEM((DEGREE, 2, 2, ROWS, FACE), BF16),
            pltpu.VMEM((DEGREE, 2, 2, ROWS, FACE), BF16),
            pltpu.VMEM((BLOCKS, PIECES, ROWS, PIECE), BF16),
            pltpu.VMEM((2, SHARED, LANES), F32),
            pltpu.VMEM((SHARED, LANES), F32),
            pltpu.VMEM((SIDE, SHARED, LANES), F32),
            pltpu.VMEM((SIDE, SHARED, LANES), F32),
            pltpu.VMEM((2, BLOCKS, SHARED, LANES), F32),
            pltpu.VMEM((ALL, ALL), F32),
            pltpu.VMEM((BLOCKS, ROWS, ALL), F32),
            dma((5,)),
            dma((2,)), dma((2,)), dma((DEGREE, 2)), dma((DEGREE, 2)),
            dma((2, BLOCKS // 2, PIECES)), dma((2, BLOCKS // 2, PIECES)),
            dma, dma,
            dma((SIDE,)), dma((SIDE,)), dma((SIDE,)), dma((SIDE,)),
            dma((BLOCKS,)), dma((BLOCKS,)), dma((BLOCKS,)), dma((BLOCKS,)),
        ],
        compiler_params=pltpu.CompilerParams(collective_id=0, has_side_effects=True),
        name="filter_and_orthonormalize",
    )(orbitals, connectivity, face_lower[None, :], face_upper[None, :], cell_matrices)


def solution(mesh):
    in_specs = (P("orb", "slab"), P("slab", None, None), P("slab", None), P("slab"), P("slab"))
    return jax.shard_map(
        per_device, mesh=mesh, in_specs=in_specs, out_specs=P("orb", "slab"), check_vma=False
    )
```
